256 devices in a mesh: prow: 32 (over y, z), pcol: 8 (over x, core).
Axes of the slice: x: 4, y: 4, z: 8, core: 2. Of those that a mesh axis runs over, the one named last changes fastest.
Arguments:
- right_side: bfloat16 [32, 6, 128, 256], P('prow'), may hold values from -6 to 6
- lower_inverse: bfloat16 [32, 6, 256, 256], P('prow'), as said below
- upper_inverse: bfloat16 [32, 6, 256, 256], P('prow'), as said below
- lower_blocks: bfloat16 [32, 5, 48, 256, 256], P('prow', None, 'pcol'), may hold values from -0.0546875 to 0.0546875
- lower_sources: int32 [32, 5, 48], P('prow', None, 'pcol'), may hold values from 0 to 159, as said below
- lower_counts: int32 [32, 5, 8], P('prow', None, 'pcol'), may hold values from 1 to 6, as said below
- upper_blocks: bfloat16 [32, 5, 48, 256, 256], P('prow', None, 'pcol'), may hold values from -0.0546875 to 0.0546875
- upper_sources: int32 [32, 5, 48], P('prow', None, 'pcol'), may hold values from 32 to 191, as said below
- upper_counts: int32 [32, 5, 8], P('prow', None, 'pcol'), may hold values from 1 to 6, as said below
Outputs:
- solution: bfloat16 [32, 6, 128, 256], P('prow')
The draws below stay inside these ranges and needn't reach their ends.
Inputs may be any that keep to these rules, and one draw needn't show every extreme that they name: `lower_sources`: entry [r, l, c] names supernode v * 32 + p of a level v below l + 1, with p % (8) == c // 6; entries may repeat. `upper_sources`: entry [r, l, c] names supernode v * 32 + p of a level v above l, with p % (8) == c // 6; entries may repeat. `lower_counts`: entry [r, l, g] is how many of the 6 slots of group g are live; the live ones come first. `upper_counts`: entry [r, l, g] is how many of the 6 slots of group g are live; the live ones come first. `lower_inverse`: each block is lower triangular. `upper_inverse`: each block is upper triangular.
All inputs are finite; a program needn't handle non-finite values.
Results may differ from the reference program's by a relative error of at most 0.02.
Values may be sent and summed in bfloat16 or wider, within the bound.
No kernel may reach another device: no remote copies, remote signals or barrier semaphores. Data moves between devices by JAX's collectives and lax.ppermute only.
A program may use at most 64 MiB of HBM per device.

```python
import jax
import jax.numpy as jnp
from jax import lax

SN = 256
NRHS = 128
LEVELS = 6
BLK_DEV = 6
W = 32
BLOCKS_ROW = 48
NS = 192


def triangle_block(key, lower):
    shape = (W, LEVELS, SN, SN)
    first, second = jax.random.split(key)
    entries = jax.random.normal(first, shape, jnp.float32)
    diagonal = jnp.exp(jax.random.uniform(second, (W, LEVELS, SN), jnp.float32, -0.7, 0.7))
    rows = jnp.arange(SN, dtype=jnp.int32)[:, None]
    cols = jnp.arange(SN, dtype=jnp.int32)[None, :]
    if lower:
        keep = rows > cols
    else:
        keep = rows < cols
    off_part = jnp.where(keep, entries * SN ** (-0.5), 0.0)
    on_part = jnp.where(rows == cols, 1.0, 0.0) * diagonal[..., None]
    return off_part + on_part


def draw_lower_inverse(key, part):
    return triangle_block(jax.random.fold_in(key, 5), True).astype(jnp.bfloat16)


def draw_upper_inverse(key, part):
    return triangle_block(jax.random.fold_in(key, 6), False).astype(jnp.bfloat16)


def source_table(key, lower):
    ncol = BLOCKS_ROW // BLK_DEV
    group = W // ncol
    shape = (W, LEVELS - 1, BLOCKS_ROW)
    first, second = jax.random.split(key)
    raw = jax.random.randint(first, shape, 0, 1 << 20)
    target = jnp.arange(0, LEVELS - 1, dtype=jnp.int32)[None, :, None]
    if lower:
        level = raw % (target + 1)
    else:
        level = target + 1 + raw % (LEVELS - 1 - target)
    column = (jnp.arange(BLOCKS_ROW, dtype=jnp.int32) // BLK_DEV)[None, None, :]
    position = column + ncol * jax.random.randint(second, shape, 0, group)
    value = level * W + position
    if lower:
        value = value.at[0, 0, 0].set(0)
        value = value.at[0, LEVELS - 2, BLOCKS_ROW - 1].set((LEVELS - 1) * W - 1)
    else:
        value = value.at[0, 0, 0].set(W)
        value = value.at[0, LEVELS - 2, BLOCKS_ROW - 1].set(NS - 1)
    return value.astype(jnp.int32)


def count_table(key):
    ncol = BLOCKS_ROW // BLK_DEV
    value = jax.random.randint(key, (W, LEVELS - 1, ncol), 1, BLK_DEV + 1)
    value = value.at[0, :, 0].set(BLK_DEV)
    value = value.at[W - 1, 0, ncol - 1].set(1)
    return value.astype(jnp.int32)


def draw_lower_sources(key, part):
    return source_table(jax.random.fold_in(key, 1), True)


def draw_lower_counts(key, part):
    return count_table(jax.random.fold_in(key, 2))


def draw_upper_sources(key, part):
    return source_table(jax.random.fold_in(key, 3), False)


def draw_upper_counts(key, part):
    return count_table(jax.random.fold_in(key, 4))


def steps_of(key, extent, cuts, low, top_value):
    def one(dim, shards_of):
        heights = jax.random.uniform(jax.random.fold_in(jax.random.fold_in(key, 6), dim), (shards_of,), jnp.float32, low / len(cuts), top_value / len(cuts))
        return jnp.repeat(jnp.exp(heights), extent[dim] // shards_of).reshape((-1,) + (1,) * (len(extent) - dim - 1))

    loudness = one(*cuts[0])
    for cut in cuts[1:]:
        loudness = loudness * one(*cut)
    return loudness


def bell_draw(key, shape, width, most, pieces=(), kind=jnp.bfloat16):
    level = steps_of(key, shape, pieces, -0.22, 0.18) if pieces else 1.0
    drawn = jax.random.normal(key, shape, jnp.float32) * width * level
    return jnp.minimum(jnp.maximum(drawn, -most), most).astype(kind)


def setup_inputs(seed: int = 0) -> dict:
    arg_keys = jax.random.split(jax.random.key(seed), 10)
    return {
        "right_side": bell_draw(arg_keys[0], (W, LEVELS, NRHS, SN), 1.0, 6.0, ((0, 32),)),
        "lower_inverse": draw_lower_inverse(jax.random.fold_in(arg_keys[9], 71), 0),
        "upper_inverse": draw_upper_inverse(jax.random.fold_in(arg_keys[9], 71), 0),
        "lower_blocks": bell_draw(arg_keys[3], (W, LEVELS - 1, BLOCKS_ROW, SN, SN), (SN * BLOCKS_ROW) ** -0.5, 0.0546875, ((0, 32), (2, 8))),
        "lower_sources": draw_lower_sources(jax.random.fold_in(arg_keys[9], 71), 0),
        "lower_counts": draw_lower_counts(jax.random.fold_in(arg_keys[9], 71), 0),
        "upper_blocks": bell_draw(arg_keys[6], (W, LEVELS - 1, BLOCKS_ROW, SN, SN), (SN * BLOCKS_ROW) ** -0.5, 0.0546875, ((0, 32), (2, 8))),
        "upper_sources": draw_upper_sources(jax.random.fold_in(arg_keys[9], 71), 0),
        "upper_counts": draw_upper_counts(jax.random.fold_in(arg_keys[9], 71), 0),
    }


def row_update(solved, blocks, sources, counts):
    slot = jnp.arange(BLOCKS_ROW, dtype=jnp.int32)

    def one_row(args):
        row_blocks, row_sources, row_counts = args
        limit = row_counts[slot // BLK_DEV]
        live = (slot % BLK_DEV) < limit
        picked = solved[row_sources].astype(jnp.float32)
        picked = jnp.where(live[:, None, None], picked, jnp.zeros_like(picked))
        return jnp.einsum("kcb,kab->ca", picked, row_blocks.astype(jnp.float32))

    return lax.map(one_row, (blocks, sources, counts))


def apply_inverse(residual, inverse):
    return jnp.einsum("rcb,rab->rca", residual.astype(jnp.float32), inverse.astype(jnp.float32)).astype(jnp.bfloat16)


def reference(right_side, lower_inverse, upper_inverse, lower_blocks, lower_sources, lower_counts, upper_blocks, upper_sources, upper_counts):
    forward = jnp.zeros((LEVELS, W, NRHS, SN), jnp.bfloat16)
    for level in range(LEVELS):
        if level == 0:
            residual = right_side[:, 0]
        else:
            update = row_update(forward.reshape(NS, NRHS, SN), lower_blocks[:, level - 1], lower_sources[:, level - 1], lower_counts[:, level - 1])
            residual = (right_side[:, level].astype(jnp.float32) - update).astype(jnp.bfloat16)
        forward = forward.at[level].set(apply_inverse(residual, lower_inverse[:, level]))
    backward = jnp.zeros((LEVELS, W, NRHS, SN), jnp.bfloat16)
    for level in range(LEVELS - 1, -1, -1):
        if level == LEVELS - 1:
            residual = forward[level]
        else:
            update = row_update(backward.reshape(NS, NRHS, SN), upper_blocks[:, level], upper_sources[:, level], upper_counts[:, level])
            residual = (forward[level].astype(jnp.float32) - update).astype(jnp.bfloat16)
        backward = backward.at[level].set(apply_inverse(residual, upper_inverse[:, level]))
    return jnp.transpose(backward, (1, 0, 2, 3))
```

```python
import functools

import jax
import jax.numpy as jnp
from jax import lax
from jax.experimental import pallas as pl
from jax.experimental.pallas import tpu as pltpu
from jax.sharding import PartitionSpec as P

BF = jnp.bfloat16
F32 = jnp.float32
NT = (((1,), (1,)), ((), ()))


def update_kernel(low, levels, width, ncol, level, sources, counts, blocks, *rest):
    stores = rest[:levels]
    out, held, sems = rest[levels:]
    slots = held.shape[0]
    count = counts[level]

    def copy(slot):
        return pltpu.make_async_copy(blocks.at[0, level, slot], held.at[slot], sems.at[slot])

    for slot in range(slots):

        @pl.when(slot < count)
        def _():
            copy(slot).start()

    out[...] = jnp.zeros_like(out)
    for slot in range(slots):

        @pl.when(slot < count)
        def _():
            copy(slot).wait()
            source = sources[level, slot]
            step = source // width - low
            place = source % width // ncol
            for v in range(levels):

                @pl.when(step == v)
                def _():
                    out[...] += lax.dot_general(stores[v][place], held[slot], NT, preferred_element_type=F32)


def update(low, stores, level, sources, counts, blocks, width, ncol):
    slots, size = blocks.shape[2], blocks.shape[3]
    nrhs = stores[0].shape[1]
    smem = pl.BlockSpec(memory_space=pltpu.SMEM)
    vmem = pl.BlockSpec(memory_space=pltpu.VMEM)
    return pl.pallas_call(
        functools.partial(update_kernel, low, len(stores), width, ncol, level),
        out_shape=jax.ShapeDtypeStruct((nrhs, size), F32),
        in_specs=[smem, smem, pl.BlockSpec(memory_space=pl.ANY)] + [vmem] * len(stores),
        out_specs=vmem,
        scratch_shapes=[pltpu.VMEM((slots, size, size), BF), pltpu.SemaphoreType.DMA((slots,))],
        name="update",
    )(sources, counts, blocks, *stores)


def finish_kernel(right, parts, inverse, out):
    total = parts[0]
    for i in range(1, parts.shape[0]):
        total = total + parts[i]
    residual = (right[...].astype(F32) - total).astype(BF)
    out[...] = lax.dot_general(residual, inverse[...], NT, preferred_element_type=F32).astype(BF)


def finish(right, parts, inverse):
    vmem = pl.BlockSpec(memory_space=pltpu.VMEM)
    return pl.pallas_call(
        finish_kernel,
        out_shape=jax.ShapeDtypeStruct(right.shape, BF),
        in_specs=[vmem] * 3,
        out_specs=vmem,
        name="finish",
    )(right, parts, inverse)


def apply_inverse(residual, inverse):
    return lax.dot_general(residual, inverse, NT, preferred_element_type=F32).astype(BF)


def shards(
    right_side,
    lower_inverse,
    upper_inverse,
    lower_blocks,
    lower_sources,
    lower_counts,
    upper_blocks,
    upper_sources,
    upper_counts,
):
    width = lax.axis_size("prow")
    ncol = lax.axis_size("pcol")
    group = width // ncol
    column = lax.axis_index("pcol")
    levels, nrhs, size = right_side.shape[1:]
    part = nrhs // ncol
    turn = [
        ((g * ncol + z) * ncol + c, (g * ncol + c) * ncol + z)
        for g in range(group)
        for z in range(ncol)
        for c in range(ncol)
    ]
    right = lax.dynamic_slice_in_dim(right_side[0], column * part, part, 1)

    def spread(solved):
        solved = lax.ppermute(solved, ("prow", "pcol"), turn)
        solved = jnp.broadcast_to(solved[None], (width, part, size))
        whole = lax.all_to_all(solved, "prow", 0, 0, tiled=True)
        return whole.reshape(group, nrhs, size)

    def reduce(partial):
        return lax.all_to_all(partial.reshape(ncol, part, size), "pcol", 0, 0, tiled=True)

    lower_args = (lower_sources[0], lower_counts[0, :, 0], lower_blocks, width, ncol)
    upper_args = (upper_sources[0], upper_counts[0, :, 0], upper_blocks, width, ncol)
    own = []
    stores = []
    for level in range(levels):
        if level == 0:
            solved = apply_inverse(right[0], lower_inverse[0, 0])
        else:
            partial = update(0, stores, level - 1, *lower_args)
            solved = finish(right[level], reduce(partial), lower_inverse[0, level])
        own.append(solved)
        if level + 1 < levels:
            stores.append(spread(solved))
    result = [None] * levels
    stores = []
    for level in range(levels - 1, -1, -1):
        if level == levels - 1:
            solved = apply_inverse(own[level], upper_inverse[0, level])
        else:
            partial = update(level + 1, stores, level, *upper_args)
            solved = finish(own[level], reduce(partial), upper_inverse[0, level])
        result[level] = solved
        if level > 0:
            stores.insert(0, spread(solved))
    whole = jnp.broadcast_to(jnp.stack(result)[None], (ncol, levels, part, size))
    whole = lax.all_to_all(whole, "pcol", 0, 0, tiled=True)
    return jnp.transpose(whole, (1, 0, 2, 3)).reshape(1, levels, nrhs, size)


def solution(mesh):
    in_specs = (
        P("prow", None, None, None),
        P("prow", None, None, None),
        P("prow", None, None, None),
        P("prow", None, "pcol", None, None),
        P("prow", None, "pcol"),
        P("prow", None, "pcol"),
        P("prow", None, "pcol", None, None),
        P("prow", None, "pcol"),
        P("prow", None, "pcol"),
    )
    out_specs = P("prow", None, None, None)
    return jax.shard_map(shards, mesh=mesh, in_specs=in_specs, out_specs=out_specs, check_vma=False)
```

```python
import functools

import jax
import jax.numpy as jnp
from jax import lax
from jax.experimental import pallas as pl
from jax.experimental.pallas import tpu as pltpu
from jax.sharding import Mesh
from jax.sharding import PartitionSpec as P

BF = jnp.bfloat16
F32 = jnp.float32
I32 = jnp.int32
NT = (((1,), (1,)), ((), ()))
ROW = ("g", "z")
TURNED = ("z", "g")
COL = ("x", "core")
SMEM = pl.BlockSpec(memory_space=pltpu.SMEM)
VMEM = pl.BlockSpec(memory_space=pltpu.VMEM)
ANY = pl.BlockSpec(memory_space=pl.ANY)
HBM = pl.BlockSpec(memory_space=pltpu.HBM)
LAST_SPLIT = 4


def dot(x, y):
    return lax.dot_general(x, y, NT, preferred_element_type=F32)


def run(copies):
    for copy in copies:
        copy.start()
    return copies


def update_kernel(level, table, blocks, *rest):
    *stores, out, held, known, sems = rest
    slots = held.shape[0]
    inputs = run([pltpu.make_async_copy(ref, known.at[i], sems.at[i]) for i, ref in enumerate(stores)])
    weights = run(
        [pltpu.make_async_copy(blocks.at[0, level, i], held.at[i], sems.at[len(stores) + i]) for i in range(slots)]
    )
    for copy in inputs:
        copy.wait()
    total = jnp.zeros(out.shape, F32)
    for slot in range(slots):
        place = table[level, slot]
        at = jnp.maximum(place, 0)
        group = known.shape[2]
        picked = known[at // group, :, at % group].reshape(out.shape)
        picked = jnp.where(place >= 0, picked, jnp.zeros_like(picked))
        weights[slot].wait()
        total += dot(picked, held[slot])
    out[...] = total


def update(level, table, blocks, stores):
    slots, size = blocks.shape[2], blocks.shape[3]
    ncol, group, part, _ = stores[0].shape
    n = len(stores)
    return pl.pallas_call(
        functools.partial(update_kernel, level),
        out_shape=jax.ShapeDtypeStruct((ncol * part, size), F32),
        in_specs=[SMEM, HBM] + [ANY] * n,
        out_specs=VMEM,
        scratch_shapes=[
            pltpu.VMEM((slots, size, size), BF),
            pltpu.VMEM((n, ncol, group, part, size), BF),
            pltpu.SemaphoreType.DMA((n + slots,)),
        ],
        compiler_params=pltpu.CompilerParams(vmem_limit_bytes=6 << 20),
        cost_estimate=pl.CostEstimate(flops=2 * slots * ncol * part * size * size, bytes_accessed=1 << 20, transcendentals=0),
        name="update",
    )(table, blocks, *stores)


def finish_kernel(level, parts, right, inverse, out, spread, held, sem):
    copy = pltpu.make_async_copy(inverse.at[0, level], held, sem)
    copy.start()
    residual = right[level]
    if parts is not None:
        total = parts[0]
        for i in range(1, parts.shape[0]):
            total = total + parts[i]
        residual = (residual.astype(F32) - total).astype(BF)
    copy.wait()
    solved = dot(residual, held[...]).astype(BF)
    out[...] = solved
    for i in range(spread.shape[0]):
        spread[i] = solved


def finish(level, parts, right, inverse, width):
    part, size = right.shape[1:]
    body = functools.partial(finish_kernel, level)
    if parts is None:
        body = functools.partial(finish_kernel, level, None)
    return pl.pallas_call(
        body,
        out_shape=[jax.ShapeDtypeStruct((part, size), BF), jax.ShapeDtypeStruct((width, part, size), BF)],
        in_specs=([] if parts is None else [VMEM]) + [VMEM, ANY],
        out_specs=[VMEM, VMEM],
        scratch_shapes=[pltpu.VMEM((size, size), BF), pltpu.SemaphoreType.DMA(())],
        compiler_params=pltpu.CompilerParams(vmem_limit_bytes=4 << 20),
        cost_estimate=pl.CostEstimate(flops=2 * part * size * size, bytes_accessed=1 << 19, transcendentals=0),
        name="finish",
    )(*([] if parts is None else [parts]), right, inverse)


def solve_kernel(n, low, row, at, levels, table, blocks, right, *rest):
    m = len(levels)
    inverses, rest = rest[:m], rest[m:]
    stores, (out, spread, held, known, diag, sems) = rest[:n], rest[n:]
    ncol, slots = held.shape[:2]
    inputs = run(
        [pltpu.make_async_copy(ref, known.at[pl.ds(i * ref.shape[0], ref.shape[0])], sems.at[i]) for i, ref in enumerate(stores)]
    )
    weights = run([pltpu.make_async_copy(blocks.at[c, at], held.at[c], sems.at[n + c]) for c in range(ncol)])
    ends = run([pltpu.make_async_copy(ref.at[0, k], diag.at[i], sems.at[n + ncol + i]) for i, (ref, k) in enumerate(zip(inverses, levels))])
    for copy in inputs:
        copy.wait()
    total = jnp.zeros(out.shape, F32)
    first = low * spread.shape[0]
    for c in range(ncol):
        weights[c].wait()
        for slot in range(slots):
            place = table[c, row * slots + slot]
            picked = known[jnp.maximum(place - first, 0)]
            picked = jnp.where(place >= 0, picked, jnp.zeros_like(picked))
            total += dot(picked, held[c, slot])
    solved = (right[...].astype(F32) - total).astype(BF)
    for i in range(m):
        ends[i].wait()
        solved = dot(solved, diag[i]).astype(BF)
    out[...] = solved
    for i in range(spread.shape[0]):
        spread[i] = solved


def solve(low, row, at, levels, table, blocks, right, inverses, stores):
    part, size = right.shape
    ncol, slots = blocks.shape[0], blocks.shape[2]
    n, m, width = len(stores), len(inverses), stores[0].shape[0]
    return pl.pallas_call(
        functools.partial(solve_kernel, n, low, row, at, levels),
        out_shape=[jax.ShapeDtypeStruct((part, size), BF), jax.ShapeDtypeStruct((width, part, size), BF)],
        in_specs=[SMEM, HBM, VMEM] + [ANY] * (m + n),
        out_specs=[VMEM, VMEM],
        scratch_shapes=[
            pltpu.VMEM((ncol, slots, size, size), BF),
            pltpu.VMEM((n * width, part, size), BF),
            pltpu.VMEM((m, size, size), BF),
            pltpu.SemaphoreType.DMA((n + ncol + m,)),
        ],
        compiler_params=pltpu.CompilerParams(vmem_limit_bytes=48 << 20),
        cost_estimate=pl.CostEstimate(flops=2 * ncol * slots * part * size * size, bytes_accessed=7 << 20, transcendentals=0),
        name="solve",
    )(table, blocks, right, *inverses, *stores)


def shards(
    right_side,
    lower_inverse,
    upper_inverse,
    lower_blocks,
    lower_sources,
    lower_counts,
    upper_blocks,
    upper_sources,
    upper_counts,
):
    width = lax.axis_size(ROW)
    ncol = lax.axis_size(COL)
    group = width // ncol
    column = lax.axis_index(COL)
    levels, nrhs, size = right_side.shape[1:]
    slots = lower_blocks.shape[2]
    part = nrhs // ncol
    right = lax.dynamic_slice_in_dim(right_side[0], column * part, part, 1)

    last = LAST_SPLIT
    low_part = lower_blocks[0, last:]
    cut = levels - 1 - (levels - 1 - low_part.shape[0] + 1) // 2
    first = jnp.concatenate([low_part, upper_blocks[0, cut:]])
    second = upper_blocks[0, :cut]
    gathered = lax.all_gather(first, COL, axis=0)
    gathered_low = lax.all_gather(second, COL, axis=0)

    def places(sources, counts, by_column):
        s, n = sources[0], counts[0]
        live = jnp.arange(slots, dtype=I32)[None] < n
        g = s % width // ncol
        place = s // width * group + g
        if by_column:
            place = (s // width * ncol + s % ncol) * group + g
        return jnp.where(live, place, -1)

    own_table = places(lower_sources, lower_counts, False)
    late = jnp.concatenate(
        [places(lower_sources, lower_counts, True)[last:], places(upper_sources, upper_counts, True)]
    ).reshape(-1)
    table = lax.all_to_all(jnp.broadcast_to(late[None], (ncol, late.shape[0])), COL, 0, 0, tiled=True)

    def spread(copies):
        return lax.all_to_all(copies, TURNED, 0, 0, tiled=True)

    def by_column(whole):
        return lax.all_to_all(whole.reshape(ncol, group, part, size), COL, 0, 0, tiled=True)

    stores, halves = [], []
    for level in range(last + 1):
        parts = None
        if level > 0:
            partial = update(level - 1, own_table, lower_blocks, halves)
            parts = lax.all_to_all(partial.reshape(ncol, part, size), COL, 0, 0, tiled=True)
        solved, copies = finish(level, parts, right, lower_inverse, width)
        if level == 0:
            own = []
        own.append(solved)
        stores.append(spread(copies))
        if level < last:
            halves.append(by_column(stores[-1]))
    nlow = low_part.shape[0]
    for level in range(last + 1, levels):
        ends = [lower_inverse], [level]
        if level == levels - 1:
            ends = [lower_inverse, upper_inverse], [level, level]
        at = level - last - 1
        solved, copies = solve(0, at, at, ends[1], table, gathered, right[level], ends[0], stores)
        own.append(solved)
        stores.append(spread(copies))
    stores = stores[-1:]
    result = [own[-1]]
    for level in range(levels - 2, -1, -1):
        blocks, at = (gathered, nlow + level - cut) if level >= cut else (gathered_low, level)
        solved, copies = solve(
            level + 1, nlow + level, at, [level], table, blocks, own[level], [upper_inverse], stores
        )
        result.insert(0, solved)
        if level > 0:
            stores.insert(0, spread(copies))
    whole = jnp.broadcast_to(jnp.stack(result)[None], (ncol, levels, part, size))
    whole = lax.all_to_all(whole, COL, 0, 0, tiled=True)
    return jnp.transpose(whole, (1, 0, 2, 3)).reshape(1, levels, nrhs, size)


def solution(mesh):
    width, ncol = mesh.devices.shape
    grid = Mesh(mesh.devices.reshape(width // ncol, ncol, ncol // 2, 2), ROW + COL)
    in_specs = (
        P(ROW, None, None, None),
        P(ROW, None, None, None),
        P(ROW, None, None, None),
        P(ROW, None, COL, None, None),
        P(ROW, None, COL),
        P(ROW, None, COL),
        P(ROW, None, COL, None, None),
        P(ROW, None, COL),
        P(ROW, None, COL),
    )
    out_specs = P(ROW, None, None, None)
    return jax.shard_map(shards, mesh=grid, in_specs=in_specs, out_specs=out_specs, check_vma=False)
```

```python
import functools

import jax
import jax.numpy as jnp
from jax import lax
from jax.experimental import pallas as pl
from jax.experimental.pallas import tpu as pltpu
from jax.sharding import Mesh
from jax.sharding import PartitionSpec as P

BF = jnp.bfloat16
F32 = jnp.float32
I32 = jnp.int32
NT = (((1,), (1,)), ((), ()))
ROW = ("g", "z")
TURNED = ("z", "g")
COL = ("x", "core")
SMEM = pl.BlockSpec(memory_space=pltpu.SMEM)
VMEM = pl.BlockSpec(memory_space=pltpu.VMEM)
ANY = pl.BlockSpec(memory_space=pl.ANY)
HBM = pl.BlockSpec(memory_space=pltpu.HBM)
LAST_SPLIT = 4
HEAD = 3


def dot(x, y):
    return lax.dot_general(x, y, NT, preferred_element_type=F32)


def run(copies):
    for copy in copies:
        copy.start()
    return copies


def params(mib):
    return pltpu.CompilerParams(vmem_limit_bytes=mib << 20)


def join_kernel(cut, low_blocks, high_blocks, out, sems):
    n = low_blocks.shape[1]
    last = n - (out.shape[0] - (high_blocks.shape[1] - cut))
    copies = [
        pltpu.make_async_copy(low_blocks.at[0, pl.ds(last, n - last)], out.at[pl.ds(0, n - last)], sems.at[0]),
        pltpu.make_async_copy(high_blocks.at[0, pl.ds(cut, n - cut)], out.at[pl.ds(n - last, n - cut)], sems.at[1]),
    ]
    for copy in run(copies):
        copy.wait()


def join(count, cut, low_blocks, high_blocks):
    return pl.pallas_call(
        functools.partial(join_kernel, cut),
        out_shape=jax.ShapeDtypeStruct((count,) + low_blocks.shape[2:], BF),
        in_specs=[ANY, ANY],
        out_specs=ANY,
        scratch_shapes=[pltpu.SemaphoreType.DMA((2,))],
        compiler_params=params(60),
        name="join",
    )(low_blocks, high_blocks)


def head_kernel(count, blocks, out, sem):
    copy = pltpu.make_async_copy(blocks.at[0, pl.ds(0, count)], out, sem)
    copy.start()
    copy.wait()


def head(count, blocks):
    return pl.pallas_call(
        functools.partial(head_kernel, count),
        out_shape=jax.ShapeDtypeStruct((count,) + blocks.shape[2:], BF),
        in_specs=[ANY],
        out_specs=ANY,
        scratch_shapes=[pltpu.SemaphoreType.DMA(())],
        compiler_params=params(60),
        name="head",
    )(blocks)


def pick(stores, first, place, load):
    width = 32
    at = jnp.maximum(place, 0)
    level, index = at // width - first, at % width
    picked = load(stores[0], index)
    for i in range(1, len(stores)):
        picked = jnp.where(level == i, load(stores[i], index), picked)
    return jnp.where(place >= 0, picked, jnp.zeros_like(picked))


def update_kernel(level, n, extra, table, blocks, *rest):
    stores, rest = rest[:n], rest[n:]
    out = rest[-1]
    ncol, group, part, size = stores[0].shape

    def load(store, index):
        return store[:, index % group].reshape(ncol * part, size)

    total = jnp.zeros((ncol * part, size), F32)
    for slot in range(blocks.shape[2]):
        total += dot(pick(stores, 0, table[level, slot], load), blocks[0, level, slot])
    out[:, :part] = total.reshape(ncol, part, size)
    if extra:
        out[:, part:] = jnp.broadcast_to(rest[0][...][None], (ncol, extra, size))


def update(level, table, blocks, stores, late=None):
    slots, size = blocks.shape[2], blocks.shape[3]
    ncol, group, part, _ = stores[0].shape
    n = len(stores)
    extra = 0 if late is None else late.shape[0]
    return pl.pallas_call(
        functools.partial(update_kernel, level, n, extra),
        out_shape=jax.ShapeDtypeStruct((ncol, part + extra, size), F32),
        in_specs=[SMEM, VMEM] + [VMEM] * (n + (late is not None)),
        out_specs=VMEM,
        compiler_params=params(4),
        cost_estimate=pl.CostEstimate(flops=2 * slots * ncol * part * size * size, bytes_accessed=1 << 20, transcendentals=0),
        name="update",
    )(table, blocks, *stores, *([] if late is None else [late]))


def finish_kernel(level, parts, right, inverse, out, spread, *table):
    residual = right[level]
    part = residual.shape[0]
    if parts is not None:
        total = parts[0, :part]
        for i in range(1, parts.shape[0]):
            total = total + parts[i, :part]
        residual = (residual.astype(F32) - total).astype(BF)
    solved = dot(residual, inverse[0, level]).astype(BF)
    out[...] = solved
    for i in range(spread.shape[0]):
        spread[i] = solved
    if table:
        for i in range(parts.shape[0]):
            table[0][i : i + 1] = parts[i, part : part + 1, :128].astype(I32)


def finish(level, parts, right, inverse, width):
    part, size = right.shape[1:]
    body = functools.partial(finish_kernel, level)
    out_shape = [jax.ShapeDtypeStruct((part, size), BF), jax.ShapeDtypeStruct((width, part, size), BF)]
    if parts is None:
        body = functools.partial(finish_kernel, level, None)
    elif parts.shape[1] > part:
        out_shape.append(jax.ShapeDtypeStruct((parts.shape[0], 128), I32))
    return pl.pallas_call(
        body,
        out_shape=out_shape,
        in_specs=([] if parts is None else [VMEM]) + [VMEM, VMEM],
        out_specs=[VMEM] * len(out_shape),
        compiler_params=params(4),
        cost_estimate=pl.CostEstimate(flops=2 * part * size * size, bytes_accessed=1 << 19, transcendentals=0),
        name="finish",
    )(*([] if parts is None else [parts]), right, inverse)


def solve_kernel(n, low, row, at, levels, held, table, blocks, right, *rest):
    m = len(levels)
    inverses, stores, rest = rest[:m], rest[m : m + n], rest[m + n :]
    ncol, _, slots = blocks.shape[:3]
    part = right.shape[0]
    copies = []
    if held:
        *rest, room, sems = rest
        copies = run([pltpu.make_async_copy(blocks.at[c, at], room.at[c], sems.at[c]) for c in range(ncol)])
    total = jnp.zeros(right.shape, F32)
    for c in range(ncol):
        if held:
            copies[c].wait()
        for slot in range(slots):
            picked = pick(stores, low, table[c, row * slots + slot], lambda store, index: store[index])
            total += dot(picked, room[c, slot] if held else blocks[c, at, slot])
    solved = (right[...].astype(F32) - total).astype(BF)
    for i, level in enumerate(levels):
        solved = dot(solved, inverses[i][0, level]).astype(BF)
    if len(rest) > 2:
        *done, out = rest
        for i in range(ncol):
            out[i, 0] = solved
            for j, ref in enumerate(done):
                out[i, j + 1] = ref[...]
    else:
        out, spread = rest
        out[...] = solved
        for i in range(spread.shape[0]):
            spread[i] = solved


def solve(low, row, at, levels, held, table, blocks, right, inverses, stores, done=()):
    part, size = right.shape
    ncol, slots = blocks.shape[0], blocks.shape[2]
    n, m, width = len(stores), len(inverses), stores[0].shape[0]
    if done:
        out_shape = jax.ShapeDtypeStruct((ncol, len(done) + 1, part, size), BF)
        out_specs = VMEM
    else:
        out_shape = [jax.ShapeDtypeStruct((part, size), BF), jax.ShapeDtypeStruct((width, part, size), BF)]
        out_specs = [VMEM, VMEM]
    scratch = [pltpu.VMEM((ncol, slots, size, size), BF), pltpu.SemaphoreType.DMA((ncol,))]
    return pl.pallas_call(
        functools.partial(solve_kernel, n, low, row, at, levels, held),
        out_shape=out_shape,
        in_specs=[SMEM, ANY if held else VMEM] + [VMEM] * (1 + m + n + len(done)),
        out_specs=out_specs,
        scratch_shapes=scratch if held else [],
        compiler_params=params(48 if held else 6),
        cost_estimate=pl.CostEstimate(flops=2 * ncol * slots * part * size * size, bytes_accessed=7 << 20, transcendentals=0),
        name="solve",
    )(table, blocks, right, *inverses, *stores, *done)


def shards(
    right_side,
    lower_inverse,
    upper_inverse,
    lower_blocks,
    lower_sources,
    lower_counts,
    upper_blocks,
    upper_sources,
    upper_counts,
):
    width = lax.axis_size(ROW)
    ncol = lax.axis_size(COL)
    group = width // ncol
    column = lax.axis_index(COL)
    levels, nrhs, size = right_side.shape[1:]
    slots = lower_blocks.shape[2]
    part = nrhs // ncol
    right = lax.dynamic_slice_in_dim(right_side[0], column * part, part, 1)

    last = LAST_SPLIT
    nlow = levels - 1 - last
    cut = HEAD
    first = join(nlow + levels - 1 - cut, cut, lower_blocks, upper_blocks)
    second = head(cut, upper_blocks)
    gathered = lax.all_gather(first, COL, axis=0)
    gathered_low = lax.all_gather(second, COL, axis=0)

    def places(sources, counts, by_column):
        s, n = sources[0], counts[0]
        live = jnp.arange(slots, dtype=I32)[None] < n
        g = s % width // ncol
        place = s // width * width + g
        if by_column:
            place = (s // width * ncol + s % ncol) * group + g
        return jnp.where(live, place, -1)

    own_table = places(lower_sources, lower_counts, False)
    late = jnp.concatenate(
        [places(lower_sources, lower_counts, True)[last:], places(upper_sources, upper_counts, True)]
    ).reshape(-1)
    late = jnp.pad(late.astype(F32)[None], ((0, 7), (0, size - late.shape[0])))

    def spread(copies):
        return lax.all_to_all(copies, TURNED, 0, 0, tiled=True)

    def by_column(whole):
        return lax.all_to_all(whole.reshape(ncol, group, part, size), COL, 0, 0, tiled=True)

    stores, halves, own = [], [], []
    for level in range(last + 1):
        parts = None
        if level > 0:
            partial = update(level - 1, own_table, lower_blocks, halves, late if level == 1 else None)
            parts = lax.all_to_all(partial, COL, 0, 0, tiled=True)
        solved, copies, *rest = finish(level, parts, right, lower_inverse, width)
        if rest:
            table = rest[0]
        own.append(solved)
        if level == last:
            copies, gathered = lax.optimization_barrier((copies, gathered))
        stores.append(spread(copies))
        if level < last:
            halves.append(by_column(stores[-1]))
    for level in range(last + 1, levels):
        ends = [lower_inverse], [level]
        if level == levels - 1:
            ends = [lower_inverse, upper_inverse], [level, level]
        at = level - last - 1
        solved, copies = solve(0, at, at, ends[1], True, table, gathered, right[level], ends[0], stores)
        own.append(solved)
        stores.append(spread(copies))
    stores = stores[-1:]
    result = [own[-1]]
    for level in range(levels - 2, -1, -1):
        blocks, at = (gathered, nlow + level - cut) if level >= cut else (gathered_low, level)
        args = (level + 1, nlow + level, at, [level], True, table, blocks, own[level], [upper_inverse], stores)
        if level > 0:
            solved, copies = solve(*args)
            result.insert(0, solved)
            stores.insert(0, spread(copies))
    whole = lax.all_to_all(solve(*args, result), COL, 0, 0, tiled=True)
    return jnp.transpose(whole, (1, 0, 2, 3)).reshape(1, levels, nrhs, size)


def solution(mesh):
    width, ncol = mesh.devices.shape
    grid = Mesh(mesh.devices.reshape(width // ncol, ncol, ncol // 2, 2), ROW + COL)
    in_specs = (
        P(ROW, None, None, None),
        P(ROW, None, None, None),
        P(ROW, None, None, None),
        P(ROW, None, COL, None, None),
        P(ROW, None, COL),
        P(ROW, None, COL),
        P(ROW, None, COL, None, None),
        P(ROW, None, COL),
        P(ROW, None, COL),
    )
    out_specs = P(ROW, None, None, None)
    return jax.shard_map(shards, mesh=grid, in_specs=in_specs, out_specs=out_specs, check_vma=False)
```

```python
import functools

import jax
import jax.numpy as jnp
from jax import lax
from jax.experimental import pallas as pl
from jax.experimental.pallas import tpu as pltpu
from jax.sharding import Mesh
from jax.sharding import PartitionSpec as P

BF = jnp.bfloat16
F32 = jnp.float32
I32 = jnp.int32
NT = (((1,), (1,)), ((), ()))
ROW = ("g", "z")
TURNED = ("z", "g")
COL = ("x", "core")
SMEM = pl.BlockSpec(memory_space=pltpu.SMEM)
VMEM = pl.BlockSpec(memory_space=pltpu.VMEM)
ANY = pl.BlockSpec(memory_space=pl.ANY)
HBM = pl.BlockSpec(memory_space=pltpu.HBM)
LAST_SPLIT = 4
HEAD = 3


def dot(x, y):
    return lax.dot_general(x, y, NT, preferred_element_type=F32)


def run(copies):
    for copy in copies:
        copy.start()
    return copies


def params(mib):
    return pltpu.CompilerParams(vmem_limit_bytes=mib << 20)


def select_kernel(parts, out, room, *sems):
    loads, stores, n = [], [], 0
    for source, low, high in parts:
        for row in range(low, high):
            loads.append(pltpu.make_async_copy(source.at[0, row], room.at[n], sems[0].at[n]))
            stores.append(pltpu.make_async_copy(room.at[n], out.at[n], sems[1].at[n]))
            n += 1
    run(loads)
    for load, store in zip(loads, stores):
        load.wait()
        store.start()
    for store in stores:
        store.wait()


def select(*parts):
    count = sum(high - low for _, low, high in parts)
    shape = parts[0][0].shape[2:]

    def body(*refs):
        n = len(parts)
        select_kernel([(ref, low, high) for ref, (_, low, high) in zip(refs, parts)], *refs[n:])

    return pl.pallas_call(
        body,
        out_shape=jax.ShapeDtypeStruct((count,) + shape, BF),
        in_specs=[ANY] * len(parts),
        out_specs=ANY,
        scratch_shapes=[
            pltpu.VMEM((count,) + shape, BF),
            pltpu.SemaphoreType.DMA((count,)),
            pltpu.SemaphoreType.DMA((count,)),
        ],
        compiler_params=params(62),
        name="select",
    )(*[source for source, _, _ in parts])


def pick(stores, first, place, load):
    width = 32
    at = jnp.maximum(place, 0)
    level, index = at // width - first, at % width
    picked = load(stores[0], index)
    for i in range(1, len(stores)):
        picked = jnp.where(level == i, load(stores[i], index), picked)
    return jnp.where(place >= 0, picked, jnp.zeros_like(picked))


def update_kernel(level, n, extra, table, blocks, *rest):
    stores, rest = rest[:n], rest[n:]
    out = rest[-1]
    ncol, group, part, size = stores[0].shape

    def load(store, index):
        return store[:, index % group].reshape(ncol * part, size)

    total = jnp.zeros((ncol * part, size), F32)
    for slot in range(blocks.shape[2]):
        total += dot(pick(stores, 0, table[level, slot], load), blocks[0, level, slot])
    out[:, :part] = total.reshape(ncol, part, size)
    if extra:
        out[:, part:] = jnp.broadcast_to(rest[0][...][None], (ncol, extra, size))


def update(level, table, blocks, stores, late=None):
    slots, size = blocks.shape[2], blocks.shape[3]
    ncol, group, part, _ = stores[0].shape
    n = len(stores)
    extra = 0 if late is None else late.shape[0]
    return pl.pallas_call(
        functools.partial(update_kernel, level, n, extra),
        out_shape=jax.ShapeDtypeStruct((ncol, part + extra, size), F32),
        in_specs=[SMEM, VMEM] + [VMEM] * (n + (late is not None)),
        out_specs=VMEM,
        compiler_params=params(4),
        cost_estimate=pl.CostEstimate(flops=2 * slots * ncol * part * size * size, bytes_accessed=1 << 20, transcendentals=0),
        name="update",
    )(table, blocks, *stores, *([] if late is None else [late]))


def finish_kernel(level, parts, right, inverse, out, spread, *table):
    residual = right[level]
    part = residual.shape[0]
    if parts is not None:
        total = parts[0, :part]
        for i in range(1, parts.shape[0]):
            total = total + parts[i, :part]
        residual = (residual.astype(F32) - total).astype(BF)
    solved = dot(residual, inverse[0, level]).astype(BF)
    out[...] = solved
    for i in range(spread.shape[0]):
        spread[i] = solved
    if table:
        for i in range(parts.shape[0]):
            table[0][i : i + 1] = parts[i, part : part + 1, :128].astype(I32)


def finish(level, parts, right, inverse, width):
    part, size = right.shape[1:]
    body = functools.partial(finish_kernel, level)
    out_shape = [jax.ShapeDtypeStruct((part, size), BF), jax.ShapeDtypeStruct((width, part, size), BF)]
    if parts is None:
        body = functools.partial(finish_kernel, level, None)
    elif parts.shape[1] > part:
        out_shape.append(jax.ShapeDtypeStruct((parts.shape[0], 128), I32))
    return pl.pallas_call(
        body,
        out_shape=out_shape,
        in_specs=([] if parts is None else [VMEM]) + [VMEM, VMEM],
        out_specs=[VMEM] * len(out_shape),
        compiler_params=params(4),
        cost_estimate=pl.CostEstimate(flops=2 * part * size * size, bytes_accessed=1 << 19, transcendentals=0),
        name="finish",
    )(*([] if parts is None else [parts]), right, inverse)


def solve_kernel(n, low, row, at, levels, held, table, blocks, right, *rest):
    m = len(levels)
    inverses, stores, rest = rest[:m], rest[m : m + n], rest[m + n :]
    ncol, _, slots = blocks.shape[:3]
    part = right.shape[0]
    copies = []
    if held:
        *rest, room, sems = rest
        copies = run([pltpu.make_async_copy(blocks.at[c, at], room.at[c], sems.at[c]) for c in range(ncol)])
    total = jnp.zeros(right.shape, F32)
    for c in range(ncol):
        if held:
            copies[c].wait()
        for slot in range(slots):
            picked = pick(stores, low, table[c, row * slots + slot], lambda store, index: store[index])
            total += dot(picked, room[c, slot] if held else blocks[c, at, slot])
    solved = (right[...].astype(F32) - total).astype(BF)
    for i, level in enumerate(levels):
        solved = dot(solved, inverses[i][0, level]).astype(BF)
    if len(rest) > 2:
        *done, out = rest
        for i in range(ncol):
            out[i, 0] = solved
            for j, ref in enumerate(done):
                out[i, j + 1] = ref[...]
    else:
        out, spread = rest
        out[...] = solved
        for i in range(spread.shape[0]):
            spread[i] = solved


def solve(low, row, at, levels, held, table, blocks, right, inverses, stores, done=()):
    part, size = right.shape
    ncol, slots = blocks.shape[0], blocks.shape[2]
    n, m, width = len(stores), len(inverses), stores[0].shape[0]
    if done:
        out_shape = jax.ShapeDtypeStruct((ncol, len(done) + 1, part, size), BF)
        out_specs = VMEM
    else:
        out_shape = [jax.ShapeDtypeStruct((part, size), BF), jax.ShapeDtypeStruct((width, part, size), BF)]
        out_specs = [VMEM, VMEM]
    scratch = [pltpu.VMEM((ncol, slots, size, size), BF), pltpu.SemaphoreType.DMA((ncol,))]
    return pl.pallas_call(
        functools.partial(solve_kernel, n, low, row, at, levels, held),
        out_shape=out_shape,
        in_specs=[SMEM, ANY if held else VMEM] + [VMEM] * (1 + m + n + len(done)),
        out_specs=out_specs,
        scratch_shapes=scratch if held else [],
        compiler_params=params(48 if held else 6),
        cost_estimate=pl.CostEstimate(flops=2 * ncol * slots * part * size * size, bytes_accessed=7 << 20, transcendentals=0),
        name="solve",
    )(table, blocks, right, *inverses, *stores, *done)


def shards(
    right_side,
    lower_inverse,
    upper_inverse,
    lower_blocks,
    lower_sources,
    lower_counts,
    upper_blocks,
    upper_sources,
    upper_counts,
):
    width = lax.axis_size(ROW)
    ncol = lax.axis_size(COL)
    group = width // ncol
    column = lax.axis_index(COL)
    levels, nrhs, size = right_side.shape[1:]
    slots = lower_blocks.shape[2]
    part = nrhs // ncol
    right = lax.dynamic_slice_in_dim(right_side[0], column * part, part, 1)

    last = LAST_SPLIT
    nlow = levels - 1 - last
    cut = HEAD
    first = select((lower_blocks, last, levels - 1), (upper_blocks, cut, levels - 1))
    second = select((upper_blocks, 0, cut))
    gathered = lax.all_gather(first, COL, axis=0)
    gathered_low = lax.all_gather(second, COL, axis=0)

    def places(sources, counts, by_column):
        s, n = sources[0], counts[0]
        live = jnp.arange(slots, dtype=I32)[None] < n
        g = s % width // ncol
        place = s // width * width + g
        if by_column:
            place = (s // width * ncol + s % ncol) * group + g
        return jnp.where(live, place, -1)

    own_table = places(lower_sources, lower_counts, False)
    late = jnp.concatenate(
        [places(lower_sources, lower_counts, True)[last:], places(upper_sources, upper_counts, True)]
    ).reshape(-1)
    late = jnp.pad(late.astype(F32)[None], ((0, 7), (0, size - late.shape[0])))

    def spread(copies):
        return lax.all_to_all(copies, TURNED, 0, 0, tiled=True)

    def by_column(whole):
        return lax.all_to_all(whole.reshape(ncol, group, part, size), COL, 0, 0, tiled=True)

    stores, halves, own = [], [], []
    for level in range(last + 1):
        parts = None
        if level > 0:
            partial = update(level - 1, own_table, lower_blocks, halves, late if level == 1 else None)
            parts = lax.all_to_all(partial, COL, 0, 0, tiled=True)
        solved, copies, *rest = finish(level, parts, right, lower_inverse, width)
        if rest:
            table = rest[0]
        own.append(solved)
        if level == last:
            copies, gathered = lax.optimization_barrier((copies, gathered))
        stores.append(spread(copies))
        if level < last:
            halves.append(by_column(stores[-1]))
    for level in range(last + 1, levels):
        ends = [lower_inverse], [level]
        if level == levels - 1:
            ends = [lower_inverse, upper_inverse], [level, level]
        at = level - last - 1
        solved, copies = solve(0, at, at, ends[1], True, table, gathered, right[level], ends[0], stores)
        own.append(solved)
        stores.append(spread(copies))
    stores = stores[-1:]
    result = [own[-1]]
    for level in range(levels - 2, -1, -1):
        blocks, at = (gathered, nlow + level - cut) if level >= cut else (gathered_low, level)
        args = (level + 1, nlow + level, at, [level], True, table, blocks, own[level], [upper_inverse], stores)
        if level > 0:
            solved, copies = solve(*args)
            result.insert(0, solved)
            stores.insert(0, spread(copies))
    whole = lax.all_to_all(solve(*args, result), COL, 0, 0, tiled=True)
    return jnp.transpose(whole, (1, 0, 2, 3)).reshape(1, levels, nrhs, size)


def solution(mesh):
    width, ncol = mesh.devices.shape
    grid = Mesh(mesh.devices.reshape(width // ncol, ncol, ncol // 2, 2), ROW + COL)
    in_specs = (
        P(ROW, None, None, None),
        P(ROW, None, None, None),
        P(ROW, None, None, None),
        P(ROW, None, COL, None, None),
        P(ROW, None, COL),
        P(ROW, None, COL),
        P(ROW, None, COL, None, None),
        P(ROW, None, COL),
        P(ROW, None, COL),
    )
    out_specs = P(ROW, None, None, None)
    return jax.shard_map(shards, mesh=grid, in_specs=in_specs, out_specs=out_specs, check_vma=False)
```

```python
import functools

import jax
import jax.numpy as jnp
from jax import lax
from jax.experimental import pallas as pl
from jax.experimental.pallas import tpu as pltpu
from jax.sharding import Mesh
from jax.sharding import PartitionSpec as P

BF = jnp.bfloat16
F32 = jnp.float32
I32 = jnp.int32
NT = (((1,), (1,)), ((), ()))
ROW = ("g", "z")
TURNED = ("z", "g")
COL = ("x", "core")
SMEM = pl.BlockSpec(memory_space=pltpu.SMEM)
VMEM = pl.BlockSpec(memory_space=pltpu.VMEM)
ANY = pl.BlockSpec(memory_space=pl.ANY)
HBM = pl.BlockSpec(memory_space=pltpu.HBM)
LAST_SPLIT = 3
RUNS = (4, 2, 1)


def dot(x, y):
    return lax.dot_general(x, y, NT, preferred_element_type=F32)


def run(copies):
    for copy in copies:
        copy.start()
    return copies


def params(mib):
    return pltpu.CompilerParams(vmem_limit_bytes=mib << 20)


def select_kernel(parts, out, room, *sems):
    loads, stores, n = [], [], 0
    for source, low, high in parts:
        for row in range(low, high):
            loads.append(pltpu.make_async_copy(source.at[0, row], room.at[n], sems[0].at[n]))
            stores.append(pltpu.make_async_copy(room.at[n], out.at[n], sems[1].at[n]))
            n += 1
    run(loads)
    for load, store in zip(loads, stores):
        load.wait()
        store.start()
    for store in stores:
        store.wait()


def select(*parts):
    count = sum(high - low for _, low, high in parts)
    shape = parts[0][0].shape[2:]

    def body(*refs):
        n = len(parts)
        select_kernel([(ref, low, high) for ref, (_, low, high) in zip(refs, parts)], *refs[n:])

    return pl.pallas_call(
        body,
        out_shape=jax.ShapeDtypeStruct((count,) + shape, BF),
        in_specs=[ANY] * len(parts),
        out_specs=ANY,
        scratch_shapes=[
            pltpu.VMEM((count,) + shape, BF),
            pltpu.SemaphoreType.DMA((count,)),
            pltpu.SemaphoreType.DMA((count,)),
        ],
        compiler_params=params(62),
        name="select",
    )(*[source for source, _, _ in parts])


def pick(stores, first, place, load):
    width = 32
    at = jnp.maximum(place, 0)
    level, index = at // width - first, at % width
    picked = load(stores[0], index)
    for i in range(1, len(stores)):
        picked = jnp.where(level == i, load(stores[i], index), picked)
    live = (place >= first * width) & (place < (first + len(stores)) * width)
    return jnp.where(live, picked, jnp.zeros_like(picked))


def update_kernel(level, n, extra, table, blocks, *rest):
    stores, rest = rest[:n], rest[n:]
    out = rest[-1]
    ncol, group, part, size = stores[0].shape

    def load(store, index):
        return store[:, index % group].reshape(ncol * part, size)

    total = jnp.zeros((ncol * part, size), F32)
    for slot in range(blocks.shape[2]):
        total += dot(pick(stores, 0, table[level, slot], load), blocks[0, level, slot])
    out[:, :part] = total.reshape(ncol, part, size)
    if extra:
        out[:, part:] = jnp.broadcast_to(rest[0][...][None], (ncol, extra, size))


def update(level, table, blocks, stores, late=None):
    slots, size = blocks.shape[2], blocks.shape[3]
    ncol, group, part, _ = stores[0].shape
    n = len(stores)
    extra = 0 if late is None else late.shape[0]
    return pl.pallas_call(
        functools.partial(update_kernel, level, n, extra),
        out_shape=jax.ShapeDtypeStruct((ncol, part + extra, size), F32),
        in_specs=[SMEM, VMEM] + [VMEM] * (n + (late is not None)),
        out_specs=VMEM,
        compiler_params=params(4),
        cost_estimate=pl.CostEstimate(flops=2 * slots * ncol * part * size * size, bytes_accessed=1 << 20, transcendentals=0),
        name="update",
    )(table, blocks, *stores, *([] if late is None else [late]))


def finish_kernel(level, parts, right, inverse, out, spread, *table):
    residual = right[level]
    part = residual.shape[0]
    if parts is not None:
        total = parts[0, :part]
        for i in range(1, parts.shape[0]):
            total = total + parts[i, :part]
        residual = (residual.astype(F32) - total).astype(BF)
    solved = dot(residual, inverse[0, level]).astype(BF)
    out[...] = solved
    for i in range(spread.shape[0]):
        spread[i] = solved
    if table:
        for i in range(parts.shape[0]):
            table[0][i : i + 1] = parts[i, part : part + 1, :128].astype(I32)


def finish(level, parts, right, inverse, width):
    part, size = right.shape[1:]
    body = functools.partial(finish_kernel, level)
    out_shape = [jax.ShapeDtypeStruct((part, size), BF), jax.ShapeDtypeStruct((width, part, size), BF)]
    if parts is None:
        body = functools.partial(finish_kernel, level, None)
    elif parts.shape[1] > part:
        out_shape.append(jax.ShapeDtypeStruct((parts.shape[0], 128), I32))
    return pl.pallas_call(
        body,
        out_shape=out_shape,
        in_specs=([] if parts is None else [VMEM]) + [VMEM, VMEM],
        out_specs=[VMEM] * len(out_shape),
        compiler_params=params(4),
        cost_estimate=pl.CostEstimate(flops=2 * part * size * size, bytes_accessed=1 << 19, transcendentals=0),
        name="finish",
    )(*([] if parts is None else [parts]), right, inverse)


def row(store, index):
    return store[index]


def hbm(blocks):
    return pltpu.with_memory_space_constraint(blocks, pltpu.HBM)


def older_kernel(first, line, at, table, blocks, *rest):
    *stores, out, room, sems = rest
    ncol, slots = room.shape[:2]
    copies = run([pltpu.make_async_copy(blocks.at[c, at], room.at[c], sems.at[c]) for c in range(ncol)])
    total = jnp.zeros(out.shape, F32)
    for c in range(ncol):
        copies[c].wait()
        for slot in range(slots):
            total += dot(pick(stores, first, table[c, line * slots + slot], row), room[c, slot])
    out[...] = total


def older(first, line, at, table, blocks, stores):
    ncol, _, slots, size, _ = blocks.shape
    part = stores[0].shape[1]
    return pl.pallas_call(
        functools.partial(older_kernel, first, line, at),
        out_shape=jax.ShapeDtypeStruct((part, size), F32),
        in_specs=[SMEM, ANY] + [VMEM] * len(stores),
        out_specs=VMEM,
        scratch_shapes=[pltpu.VMEM((ncol, slots, size, size), BF), pltpu.SemaphoreType.DMA((ncol,))],
        compiler_params=params(10),
        cost_estimate=pl.CostEstimate(flops=2 * ncol * slots * part * size * size, bytes_accessed=13 << 20, transcendentals=0),
        name="older",
    )(table, hbm(blocks), *stores)


def solve_kernel(newest, line, at, levels, olds, table, blocks, store, right, *rest):
    m = len(levels)
    before, rest = rest[:olds], rest[olds:]
    inverses, rest = rest[:m], rest[m:]
    *rest, found, room, sems = rest
    ncol, slots = blocks.shape[0], blocks.shape[2]

    def fetch(code, j):
        i = code // 32
        return pltpu.make_async_copy(blocks.at[i // slots, at, i % slots], room.at[j], sems.at[j])

    n = jnp.int32(0)
    for i in range(ncol * slots):
        place = table[i // slots, line * slots + i % slots]
        found[n] = i * 32 + place % 32
        n = n + jnp.where((place >= newest * 32) & (place < newest * 32 + 32), 1, 0)

    @pl.loop(0, n)
    def _(j):
        fetch(found[j], j).start()

    def one(j, total):
        code = found[j]
        fetch(code, j).wait()
        return total + dot(store[code % 32], room[j])

    total = before[0][...] if olds else jnp.zeros(right.shape, F32)
    total = lax.fori_loop(0, n, one, total)
    solved = (right[...].astype(F32) - total).astype(BF)
    for i, level in enumerate(levels):
        solved = dot(solved, inverses[i][0, level]).astype(BF)
    if len(rest) > 2:
        *done, out = rest
        for i in range(ncol):
            out[i, 0] = solved
            for j, ref in enumerate(done):
                out[i, j + 1] = ref[...]
    else:
        out, spread = rest
        out[...] = solved
        for i in range(spread.shape[0]):
            spread[i] = solved


def solve(newest, line, at, levels, table, blocks, store, right, before, inverses, done=()):
    part, size = right.shape
    ncol, slots = blocks.shape[0], blocks.shape[2]
    width = store.shape[0]
    if done:
        out_shape = jax.ShapeDtypeStruct((ncol, len(done) + 1, part, size), BF)
        out_specs = VMEM
    else:
        out_shape = [jax.ShapeDtypeStruct((part, size), BF), jax.ShapeDtypeStruct((width, part, size), BF)]
        out_specs = [VMEM, VMEM]
    return pl.pallas_call(
        functools.partial(solve_kernel, newest, line, at, levels, len(before)),
        out_shape=out_shape,
        in_specs=[SMEM, ANY] + [VMEM] * (2 + len(before) + len(inverses) + len(done)),
        out_specs=out_specs,
        scratch_shapes=[
            pltpu.SMEM((ncol * slots + 1,), I32),
            pltpu.VMEM((ncol * slots, size, size), BF),
            pltpu.SemaphoreType.DMA((ncol * slots,)),
        ],
        compiler_params=params(10),
        cost_estimate=pl.CostEstimate(flops=2 * ncol * slots * part * size * size, bytes_accessed=4 << 20, transcendentals=0),
        name="solve",
    )(table, hbm(blocks), store, right, *before, *inverses, *done)


def shards(
    right_side,
    lower_inverse,
    upper_inverse,
    lower_blocks,
    lower_sources,
    lower_counts,
    upper_blocks,
    upper_sources,
    upper_counts,
):
    width = lax.axis_size(ROW)
    ncol = lax.axis_size(COL)
    group = width // ncol
    column = lax.axis_index(COL)
    levels, nrhs, size = right_side.shape[1:]
    slots = lower_blocks.shape[2]
    part = nrhs // ncol
    right = lax.dynamic_slice_in_dim(right_side[0], column * part, part, 1)

    last = LAST_SPLIT
    late_rows = [(lower_blocks, level - 1) for level in range(last + 1, levels)]
    late_rows += [(upper_blocks, level) for level in range(levels - 2, -1, -1)]
    gathered, begin = [], 0
    for count in RUNS:
        rows = select(*[(source, k, k + 1) for source, k in late_rows[begin : begin + count]])
        whole = lax.all_gather(rows, COL, axis=0)
        gathered += [(whole, i) for i in range(count)]
        begin += count

    def places(sources, counts, by_column):
        s, n = sources[0], counts[0]
        live = jnp.arange(slots, dtype=I32)[None] < n
        g = s % width // ncol
        place = s // width * width + g
        if by_column:
            place = (s // width * ncol + s % ncol) * group + g
        return jnp.where(live, place, -1)

    own_table = places(lower_sources, lower_counts, False)
    late = jnp.concatenate(
        [
            places(lower_sources, lower_counts, True)[last:],
            places(upper_sources, upper_counts, True)[::-1],
        ]
    ).reshape(-1)
    late = jnp.pad(late.astype(F32)[None], ((0, 7), (0, size - late.shape[0])))

    def spread(copies):
        return lax.all_to_all(copies, TURNED, 0, 0, tiled=True)

    def by_column(whole):
        return lax.all_to_all(whole.reshape(ncol, group, part, size), COL, 0, 0, tiled=True)

    stores, halves, own = [], [], []
    for level in range(last + 1):
        parts = None
        if level > 0:
            partial = update(level - 1, own_table, lower_blocks, halves, late if level == 1 else None)
            parts = lax.all_to_all(partial, COL, 0, 0, tiled=True)
        solved, copies, *rest = finish(level, parts, right, lower_inverse, width)
        if rest:
            table = rest[0]
        own.append(solved)
        if level < last:
            stores.append(spread(copies))
            halves.append(by_column(stores[-1]))

    def step(line, olds, first, copies):
        blocks, at = gathered[line]
        copies, tied = lax.optimization_barrier((copies, table))
        before = [older(first, line, at, tied, blocks, olds)] if olds else []
        return spread(copies), before

    line = 0
    for level in range(last + 1, levels):
        newest, before = step(line, stores, 0, copies)
        ends = [lower_inverse], [level]
        if level == levels - 1:
            ends = [lower_inverse, upper_inverse], [level, level]
        blocks, at = gathered[line]
        solved, copies = solve(level - 1, line, at, ends[1], table, blocks, newest, right[level], before, ends[0])
        own.append(solved)
        stores.append(newest)
        line += 1
    result, stores = [solved], []
    for level in range(levels - 2, -1, -1):
        newest, before = step(line, stores, level + 2, copies)
        blocks, at = gathered[line]
        done = result if level == 0 else ()
        solved = solve(level + 1, line, at, [level], table, blocks, newest, own[level], before, [upper_inverse], done)
        if level > 0:
            solved, copies = solved
            result.insert(0, solved)
            stores.insert(0, newest)
        line += 1
    whole = lax.all_to_all(solved, COL, 0, 0, tiled=True)
    return jnp.transpose(whole, (1, 0, 2, 3)).reshape(1, levels, nrhs, size)


def solution(mesh):
    width, ncol = mesh.devices.shape
    grid = Mesh(mesh.devices.reshape(width // ncol, ncol, ncol // 2, 2), ROW + COL)
    in_specs = (
        P(ROW, None, None, None),
        P(ROW, None, None, None),
        P(ROW, None, None, None),
        P(ROW, None, COL, None, None),
        P(ROW, None, COL),
        P(ROW, None, COL),
        P(ROW, None, COL, None, None),
        P(ROW, None, COL),
        P(ROW, None, COL),
    )
    out_specs = P(ROW, None, None, None)
    return jax.shard_map(shards, mesh=grid, in_specs=in_specs, out_specs=out_specs, check_vma=False)
```

```python
import functools

import jax
import jax.numpy as jnp
from jax import lax
from jax.experimental import pallas as pl
from jax.experimental.pallas import tpu as pltpu
from jax.sharding import Mesh
from jax.sharding import PartitionSpec as P

BF = jnp.bfloat16
F32 = jnp.float32
I32 = jnp.int32
NT = (((1,), (1,)), ((), ()))
ROW = ("g", "z")
TURNED = ("z", "g")
COL = ("x", "core")
SMEM = pl.BlockSpec(memory_space=pltpu.SMEM)
VMEM = pl.BlockSpec(memory_space=pltpu.VMEM)
ANY = pl.BlockSpec(memory_space=pl.ANY)
HBM = pl.BlockSpec(memory_space=pltpu.HBM)
LAST_SPLIT = 3
RUNS = (4, 2, 1)
STEP = 4


def dot(x, y):
    return lax.dot_general(x, y, NT, preferred_element_type=F32)


def run(copies):
    for copy in copies:
        copy.start()
    return copies


def params(mib):
    return pltpu.CompilerParams(vmem_limit_bytes=mib << 20)


def select_kernel(parts, out, room, *sems):
    loads, stores, n = [], [], 0
    for source, low, high in parts:
        for row in range(low, high):
            loads.append(pltpu.make_async_copy(source.at[0, row], room.at[n], sems[0].at[n]))
            stores.append(pltpu.make_async_copy(room.at[n], out.at[n], sems[1].at[n]))
            n += 1
    run(loads)
    for load, store in zip(loads, stores):
        load.wait()
        store.start()
    for store in stores:
        store.wait()


def select(*parts):
    count = sum(high - low for _, low, high in parts)
    shape = parts[0][0].shape[2:]

    def body(*refs):
        n = len(parts)
        select_kernel([(ref, low, high) for ref, (_, low, high) in zip(refs, parts)], *refs[n:])

    return pl.pallas_call(
        body,
        out_shape=jax.ShapeDtypeStruct((count,) + shape, BF),
        in_specs=[ANY] * len(parts),
        out_specs=ANY,
        scratch_shapes=[
            pltpu.VMEM((count,) + shape, BF),
            pltpu.SemaphoreType.DMA((count,)),
            pltpu.SemaphoreType.DMA((count,)),
        ],
        compiler_params=params(62),
        name="select",
    )(*[source for source, _, _ in parts])


def pick(stores, first, place, load):
    width = 32
    at = jnp.maximum(place, 0)
    level, index = at // width - first, at % width
    picked = load(stores[0], index)
    for i in range(1, len(stores)):
        picked = jnp.where(level == i, load(stores[i], index), picked)
    live = (place >= first * width) & (place < (first + len(stores)) * width)
    return jnp.where(live, picked, jnp.zeros_like(picked))


def update_kernel(level, n, extra, table, blocks, *rest):
    stores, rest = rest[:n], rest[n:]
    out = rest[-1]
    ncol, group, part, size = stores[0].shape

    def load(store, index):
        return store[:, index % group].reshape(ncol * part, size)

    total = jnp.zeros((ncol * part, size), F32)
    for slot in range(blocks.shape[2]):
        total += dot(pick(stores, 0, table[level, slot], load), blocks[0, level, slot])
    out[:, :part] = total.reshape(ncol, part, size)
    if extra:
        out[:, part:] = jnp.broadcast_to(rest[0][...][None], (ncol, extra, size))


def update(level, table, blocks, stores, late=None):
    slots, size = blocks.shape[2], blocks.shape[3]
    ncol, group, part, _ = stores[0].shape
    n = len(stores)
    extra = 0 if late is None else late.shape[0]
    return pl.pallas_call(
        functools.partial(update_kernel, level, n, extra),
        out_shape=jax.ShapeDtypeStruct((ncol, part + extra, size), F32),
        in_specs=[SMEM, VMEM] + [VMEM] * (n + (late is not None)),
        out_specs=VMEM,
        compiler_params=params(4),
        cost_estimate=pl.CostEstimate(flops=2 * slots * ncol * part * size * size, bytes_accessed=1 << 20, transcendentals=0),
        name="update",
    )(table, blocks, *stores, *([] if late is None else [late]))


def finish_kernel(level, parts, right, inverse, out, spread, *table):
    residual = right[level]
    part = residual.shape[0]
    if parts is not None:
        total = parts[0, :part]
        for i in range(1, parts.shape[0]):
            total = total + parts[i, :part]
        residual = (residual.astype(F32) - total).astype(BF)
    solved = dot(residual, inverse[0, level]).astype(BF)
    out[...] = solved
    for i in range(spread.shape[0]):
        spread[i] = solved
    if table:
        for i in range(parts.shape[0]):
            table[0][i : i + 1] = parts[i, part : part + 1, :128].astype(I32)


def finish(level, parts, right, inverse, width):
    part, size = right.shape[1:]
    body = functools.partial(finish_kernel, level)
    out_shape = [jax.ShapeDtypeStruct((part, size), BF), jax.ShapeDtypeStruct((width, part, size), BF)]
    if parts is None:
        body = functools.partial(finish_kernel, level, None)
    elif parts.shape[1] > part:
        out_shape.append(jax.ShapeDtypeStruct((parts.shape[0], 128), I32))
    return pl.pallas_call(
        body,
        out_shape=out_shape,
        in_specs=([] if parts is None else [VMEM]) + [VMEM, VMEM],
        out_specs=[VMEM] * len(out_shape),
        compiler_params=params(4),
        cost_estimate=pl.CostEstimate(flops=2 * part * size * size, bytes_accessed=1 << 19, transcendentals=0),
        name="finish",
    )(*([] if parts is None else [parts]), right, inverse)


def row(store, index):
    return store[index]


def hbm(blocks):
    return pltpu.with_memory_space_constraint(blocks, pltpu.HBM)


def older_kernel(first, line, at, table, blocks, *rest):
    *stores, out, room, sems = rest
    ncol, slots = room.shape[:2]
    copies = run([pltpu.make_async_copy(blocks.at[c, at], room.at[c], sems.at[c]) for c in range(ncol)])
    total = jnp.zeros(out.shape, F32)
    for c in range(ncol):
        copies[c].wait()
        for slot in range(slots):
            total += dot(pick(stores, first, table[c, line * slots + slot], row), room[c, slot])
    out[...] = total


def older(first, line, at, table, blocks, stores):
    ncol, _, slots, size, _ = blocks.shape
    part = stores[0].shape[1]
    return pl.pallas_call(
        functools.partial(older_kernel, first, line, at),
        out_shape=jax.ShapeDtypeStruct((part, size), F32),
        in_specs=[SMEM, ANY] + [VMEM] * len(stores),
        out_specs=VMEM,
        scratch_shapes=[pltpu.VMEM((ncol, slots, size, size), BF), pltpu.SemaphoreType.DMA((ncol,))],
        compiler_params=params(10),
        cost_estimate=pl.CostEstimate(flops=2 * ncol * slots * part * size * size, bytes_accessed=13 << 20, transcendentals=0),
        name="older",
    )(table, hbm(blocks), *stores)


def solve_kernel(newest, line, at, levels, olds, table, blocks, store, right, *rest):
    m = len(levels)
    before, rest = rest[:olds], rest[olds:]
    inverses, rest = rest[:m], rest[m:]
    *rest, found, room, sems = rest
    ncol, slots = blocks.shape[0], blocks.shape[2]
    if olds:
        n = jnp.int32(0)
        for i in range(ncol * slots):
            place = table[i // slots, line * slots + i % slots]
            hit = (place >= newest * 32) & (place < newest * 32 + 32)

            @pl.when(hit)
            def _():
                pltpu.make_async_copy(blocks.at[i // slots, at, i % slots], room.at[n], sems.at[n]).start()
                found[n] = place - newest * 32

            n = n + jnp.where(hit, 1, 0)

        def some(k, total):
            for u in range(STEP):
                j = k * STEP + u

                @pl.when(j < n)
                def _():
                    pltpu.make_async_copy(blocks.at[0, at, 0], room.at[j], sems.at[j]).wait()

            terms = []
            for u in range(STEP):
                j = k * STEP + u
                to = jnp.minimum(j, n - 1)
                picked = store[found[to]]
                picked = jnp.where(j < n, picked, jnp.zeros_like(picked))
                terms.append(dot(picked, room[to]))
            while len(terms) > 1:
                terms = [x + y for x, y in zip(terms[::2], terms[1::2])]
            return total + terms[0]

        total = lax.fori_loop(0, (n + STEP - 1) // STEP, some, before[0][...])
    else:
        copies = run(
            [
                pltpu.make_async_copy(blocks.at[c, at], room.at[pl.ds(c * slots, slots)], sems.at[c])
                for c in range(ncol)
            ]
        )
        total = jnp.zeros(right.shape, F32)
        for c in range(ncol):
            copies[c].wait()
            for slot in range(slots):
                picked = pick([store], newest, table[c, line * slots + slot], row)
                total += dot(picked, room[c * slots + slot])
    solved = (right[...].astype(F32) - total).astype(BF)
    for i, level in enumerate(levels):
        solved = dot(solved, inverses[i][0, level]).astype(BF)
    if len(rest) > 2:
        *done, out = rest
        for i in range(ncol):
            out[i, 0] = solved
            for j, ref in enumerate(done):
                out[i, j + 1] = ref[...]
    else:
        out, spread = rest
        out[...] = solved
        for i in range(spread.shape[0]):
            spread[i] = solved


def solve(newest, line, at, levels, table, blocks, store, right, before, inverses, done=()):
    part, size = right.shape
    ncol, slots = blocks.shape[0], blocks.shape[2]
    width = store.shape[0]
    if done:
        out_shape = jax.ShapeDtypeStruct((ncol, len(done) + 1, part, size), BF)
        out_specs = VMEM
    else:
        out_shape = [jax.ShapeDtypeStruct((part, size), BF), jax.ShapeDtypeStruct((width, part, size), BF)]
        out_specs = [VMEM, VMEM]
    return pl.pallas_call(
        functools.partial(solve_kernel, newest, line, at, levels, len(before)),
        out_shape=out_shape,
        in_specs=[SMEM, ANY] + [VMEM] * (2 + len(before) + len(inverses) + len(done)),
        out_specs=out_specs,
        scratch_shapes=[
            pltpu.SMEM((ncol * slots + 1,), I32),
            pltpu.VMEM((ncol * slots, size, size), BF),
            pltpu.SemaphoreType.DMA((ncol * slots,)),
        ],
        compiler_params=params(10),
        cost_estimate=pl.CostEstimate(flops=2 * ncol * slots * part * size * size, bytes_accessed=4 << 20, transcendentals=0),
        name="solve",
    )(table, hbm(blocks), store, right, *before, *inverses, *done)


def shards(
    right_side,
    lower_inverse,
    upper_inverse,
    lower_blocks,
    lower_sources,
    lower_counts,
    upper_blocks,
    upper_sources,
    upper_counts,
):
    width = lax.axis_size(ROW)
    ncol = lax.axis_size(COL)
    group = width // ncol
    column = lax.axis_index(COL)
    levels, nrhs, size = right_side.shape[1:]
    slots = lower_blocks.shape[2]
    part = nrhs // ncol
    right = lax.dynamic_slice_in_dim(right_side[0], column * part, part, 1)

    last = LAST_SPLIT
    late_rows = [(lower_blocks, level - 1) for level in range(last + 1, levels)]
    late_rows += [(upper_blocks, level) for level in range(levels - 2, -1, -1)]
    gathered = []

    def gather(count, tie=None):
        rows = late_rows[len(gathered) : len(gathered) + count]
        if tie is not None:
            tie, high = lax.optimization_barrier((tie, upper_blocks))
            rows = [(high, k) for _, k in rows]
        whole = lax.all_gather(select(*[(source, k, k + 1) for source, k in rows]), COL, axis=0)
        gathered.extend((whole, i) for i in range(count))
        return tie

    gather(RUNS[0])

    def places(sources, counts, by_column):
        s, n = sources[0], counts[0]
        live = jnp.arange(slots, dtype=I32)[None] < n
        g = s % width // ncol
        place = s // width * width + g
        if by_column:
            place = (s // width * ncol + s % ncol) * group + g
        return jnp.where(live, place, -1)

    own_table = places(lower_sources, lower_counts, False)
    late = jnp.concatenate(
        [
            places(lower_sources, lower_counts, True)[last:],
            places(upper_sources, upper_counts, True)[::-1],
        ]
    ).reshape(-1)
    late = jnp.pad(late.astype(F32)[None], ((0, 7), (0, size - late.shape[0])))

    def spread(copies):
        return lax.all_to_all(copies, TURNED, 0, 0, tiled=True)

    def by_column(whole):
        return lax.all_to_all(whole.reshape(ncol, group, part, size), COL, 0, 0, tiled=True)

    stores, halves, own = [], [], []
    for level in range(last + 1):
        parts = None
        if level > 0:
            partial = update(level - 1, own_table, lower_blocks, halves, late if level == 1 else None)
            parts = lax.all_to_all(partial, COL, 0, 0, tiled=True)
        solved, copies, *rest = finish(level, parts, right, lower_inverse, width)
        if rest:
            table = rest[0]
        own.append(solved)
        if level == 0:
            for count in RUNS[1:]:
                copies = gather(count, copies)
        if level < last:
            stores.append(spread(copies))
            halves.append(by_column(stores[-1]))

    def step(line, olds, first, copies):
        blocks, at = gathered[line]
        copies, tied = lax.optimization_barrier((copies, table))
        before = [older(first, line, at, tied, blocks, olds)] if olds else []
        return spread(copies), before

    line = 0
    for level in range(last + 1, levels):
        newest, before = step(line, stores, 0, copies)
        ends = [lower_inverse], [level]
        if level == levels - 1:
            ends = [lower_inverse, upper_inverse], [level, level]
        blocks, at = gathered[line]
        solved, copies = solve(level - 1, line, at, ends[1], table, blocks, newest, right[level], before, ends[0])
        own.append(solved)
        stores.append(newest)
        line += 1
    result, stores = [solved], []
    for level in range(levels - 2, -1, -1):
        newest, before = step(line, stores, level + 2, copies)
        blocks, at = gathered[line]
        done = result if level == 0 else ()
        solved = solve(level + 1, line, at, [level], table, blocks, newest, own[level], before, [upper_inverse], done)
        if level > 0:
            solved, copies = solved
            result.insert(0, solved)
            stores.insert(0, newest)
        line += 1
    whole = lax.all_to_all(solved, COL, 0, 0, tiled=True)
    return jnp.transpose(whole, (1, 0, 2, 3)).reshape(1, levels, nrhs, size)


def solution(mesh):
    width, ncol = mesh.devices.shape
    grid = Mesh(mesh.devices.reshape(width // ncol, ncol, ncol // 2, 2), ROW + COL)
    in_specs = (
        P(ROW, None, None, None),
        P(ROW, None, None, None),
        P(ROW, None, None, None),
        P(ROW, None, COL, None, None),
        P(ROW, None, COL),
        P(ROW, None, COL),
        P(ROW, None, COL, None, None),
        P(ROW, None, COL),
        P(ROW, None, COL),
    )
    out_specs = P(ROW, None, None, None)
    return jax.shard_map(shards, mesh=grid, in_specs=in_specs, out_specs=out_specs, check_vma=False)
```

```python
import functools

import jax
import jax.numpy as jnp
from jax import lax
from jax.experimental import pallas as pl
from jax.experimental.pallas import tpu as pltpu
from jax.sharding import Mesh
from jax.sharding import PartitionSpec as P

BF = jnp.bfloat16
F32 = jnp.float32
I32 = jnp.int32
NT = (((1,), (1,)), ((), ()))
ROW = ("g", "z")
TURNED = ("z", "g")
COL = ("x", "core")
SMEM = pl.BlockSpec(memory_space=pltpu.SMEM)
VMEM = pl.BlockSpec(memory_space=pltpu.VMEM)
ANY = pl.BlockSpec(memory_space=pl.ANY)
HBM = pl.BlockSpec(memory_space=pltpu.HBM)
LAST_SPLIT = 3
RUNS = (4, 2, 1)
STEP = 4
READY = (6, 10)


def dot(x, y):
    return lax.dot_general(x, y, NT, preferred_element_type=F32)


def run(copies):
    for copy in copies:
        copy.start()
    return copies


def params(mib):
    return pltpu.CompilerParams(vmem_limit_bytes=mib << 20)


def hbm(blocks):
    return pltpu.with_memory_space_constraint(blocks, pltpu.HBM)


def begin_kernel(lines, runs, column, low_blocks, high_blocks, right_side, inverse, *rest):
    outs, rest = rest[: len(runs)], rest[len(runs) :]
    right, out, spread, diag, room, loads, stores, sems = rest
    part = right.shape[1]
    start = pl.multiple_of(column[0] * part, part)
    small = run(
        [
            pltpu.make_async_copy(right_side.at[0, :, pl.ds(start, part)], right, sems.at[0]),
            pltpu.make_async_copy(inverse.at[0, 0], diag, sems.at[1]),
        ]
    )
    sources = (low_blocks, high_blocks)
    reads = run(
        [pltpu.make_async_copy(sources[which].at[0, k], room.at[i], loads.at[i]) for i, (which, k) in enumerate(lines)]
    )
    places = [(j, i) for j, count in enumerate(runs) for i in range(count)]
    writes = [pltpu.make_async_copy(room.at[n], outs[j].at[i], stores.at[n]) for n, (j, i) in enumerate(places)]
    for copy in small:
        copy.wait()
    solved = dot(right[0], diag[...]).astype(BF)
    out[...] = solved
    for i in range(spread.shape[0]):
        spread[i] = solved
    for read, write in zip(reads, writes):
        read.wait()
        write.start()
    for write in writes:
        write.wait()


def begin(lines, runs, column, low_blocks, high_blocks, right_side, inverse, ncol, width):
    block = low_blocks.shape[2:]
    levels, nrhs, size = right_side.shape[1:]
    part = nrhs // ncol
    n = len(lines)
    return pl.pallas_call(
        functools.partial(begin_kernel, lines, runs),
        out_shape=[pltpu.HBM((count,) + block, BF) for count in runs]
        + [jax.ShapeDtypeStruct(shape, BF) for shape in ((levels, part, size), (part, size), (width, part, size))],
        in_specs=[SMEM] + [ANY] * 4,
        out_specs=[ANY] * len(runs) + [VMEM] * 3,
        scratch_shapes=[
            pltpu.VMEM((size, size), BF),
            pltpu.VMEM((n,) + block, BF),
            pltpu.SemaphoreType.DMA((n,)),
            pltpu.SemaphoreType.DMA((n,)),
            pltpu.SemaphoreType.DMA((2,)),
        ],
        compiler_params=params(10),
        name="begin",
    )(column, hbm(low_blocks), hbm(high_blocks), hbm(right_side), hbm(inverse))


def pick(stores, first, place, load):
    width = 32
    at = jnp.maximum(place, 0)
    level, index = at // width - first, at % width
    picked = load(stores[0], index)
    for i in range(1, len(stores)):
        picked = jnp.where(level == i, load(stores[i], index), picked)
    live = (place >= first * width) & (place < (first + len(stores)) * width)
    return jnp.where(live, picked, jnp.zeros_like(picked))


def update_kernel(level, n, extra, table, blocks, *rest):
    stores, rest = rest[:n], rest[n:]
    out = rest[-1]
    ncol, group, part, size = stores[0].shape

    def load(store, index):
        return store[:, index % group].reshape(ncol * part, size)

    total = jnp.zeros((ncol * part, size), F32)
    for slot in range(blocks.shape[2]):
        total += dot(pick(stores, 0, table[level, slot], load), blocks[0, level, slot])
    out[:, :part] = total.reshape(ncol, part, size)
    if extra:
        out[:, part:] = jnp.broadcast_to(rest[0][...][None], (ncol, extra, size))


def update(level, table, blocks, stores, late=None):
    slots, size = blocks.shape[2], blocks.shape[3]
    ncol, group, part, _ = stores[0].shape
    n = len(stores)
    extra = 0 if late is None else late.shape[0]
    return pl.pallas_call(
        functools.partial(update_kernel, level, n, extra),
        out_shape=jax.ShapeDtypeStruct((ncol, part + extra, size), F32),
        in_specs=[SMEM, VMEM] + [VMEM] * (n + (late is not None)),
        out_specs=VMEM,
        compiler_params=params(4),
        cost_estimate=pl.CostEstimate(flops=2 * slots * ncol * part * size * size, bytes_accessed=1 << 20, transcendentals=0),
        name="update",
    )(table, blocks, *stores, *([] if late is None else [late]))


def finish_kernel(level, parts, right, inverse, out, spread, *table):
    residual = right[level]
    part = residual.shape[0]
    if parts is not None:
        total = parts[0, :part]
        for i in range(1, parts.shape[0]):
            total = total + parts[i, :part]
        residual = (residual.astype(F32) - total).astype(BF)
    solved = dot(residual, inverse[0, level]).astype(BF)
    out[...] = solved
    for i in range(spread.shape[0]):
        spread[i] = solved
    if table:
        for i in range(parts.shape[0]):
            table[0][i : i + 1] = parts[i, part : part + 1, :128].astype(I32)


def finish(level, parts, right, inverse, width):
    part, size = right.shape[1:]
    body = functools.partial(finish_kernel, level)
    out_shape = [jax.ShapeDtypeStruct((part, size), BF), jax.ShapeDtypeStruct((width, part, size), BF)]
    if parts is None:
        body = functools.partial(finish_kernel, level, None)
    elif parts.shape[1] > part:
        out_shape.append(jax.ShapeDtypeStruct((parts.shape[0], 128), I32))
    return pl.pallas_call(
        body,
        out_shape=out_shape,
        in_specs=([] if parts is None else [VMEM]) + [VMEM, VMEM],
        out_specs=[VMEM] * len(out_shape),
        compiler_params=params(4),
        cost_estimate=pl.CostEstimate(flops=2 * part * size * size, bytes_accessed=1 << 19, transcendentals=0),
        name="finish",
    )(*([] if parts is None else [parts]), right, inverse)


def row(store, index):
    return store[index]


def older_kernel(first, line, at, newest, table, blocks, *rest):
    *stores, out, found, ready, room, sems, ready_sems = rest
    ncol, slots = room.shape[:2]
    cap = ready.shape[0]
    copies = run([pltpu.make_async_copy(blocks.at[c, at], room.at[c], sems.at[c]) for c in range(ncol)])
    n = jnp.int32(0)
    for i in range(ncol * slots):
        place = table[i // slots, line * slots + i % slots]
        hit = (place >= newest * 32) & (place < newest * 32 + 32)

        @pl.when(hit)
        def _():
            found[n] = i * 32 + place - newest * 32

        n = n + jnp.where(hit, 1, 0)
    found[ncol * slots] = n
    total = jnp.zeros(out.shape, F32)
    for c in range(ncol):
        copies[c].wait()
        for slot in range(slots):
            total += dot(pick(stores, first, table[c, line * slots + slot], row), room[c, slot])
    out[...] = total

    def keep(j, _):
        i = found[j] // 32
        copy = pltpu.make_async_copy(room.at[i // slots, i % slots], ready.at[j], ready_sems.at[j])
        copy.start()
        return _

    def kept(j, _):
        pltpu.make_async_copy(room.at[0, 0], ready.at[j], ready_sems.at[j]).wait()
        return _

    lax.fori_loop(0, jnp.minimum(n, cap), keep, 0)
    lax.fori_loop(0, jnp.minimum(n, cap), kept, 0)


def older(ready, first, line, at, newest, table, blocks, stores):
    ncol, _, slots, size, _ = blocks.shape
    part = stores[0].shape[1]
    return pl.pallas_call(
        functools.partial(older_kernel, first, line, at, newest),
        out_shape=[
            pltpu.VMEM((part, size), F32),
            jax.ShapeDtypeStruct((64,), I32),
            pltpu.VMEM((ready, size, size), BF),
        ],
        in_specs=[SMEM, ANY] + [VMEM] * len(stores),
        out_specs=[VMEM, SMEM, VMEM],
        scratch_shapes=[
            pltpu.VMEM((ncol, slots, size, size), BF),
            pltpu.SemaphoreType.DMA((ncol,)),
            pltpu.SemaphoreType.DMA((ready,)),
        ],
        compiler_params=params(10),
        cost_estimate=pl.CostEstimate(flops=2 * ncol * slots * part * size * size, bytes_accessed=13 << 20, transcendentals=0),
        name="older",
    )(table, hbm(blocks), *stores)


def finish_row(total, right, level, inverses, levels, rest):
    solved = ((right[level] if len(right.shape) > 2 else right[...]).astype(F32) - total).astype(BF)
    for i, level in enumerate(levels):
        solved = dot(solved, inverses[i][0, level]).astype(BF)
    if len(rest) > 2:
        *done, out = rest
        for i in range(out.shape[0]):
            out[i, 0] = solved
            for j, ref in enumerate(done):
                out[i, j + 1] = ref[...]
    else:
        out, spread = rest
        out[...] = solved
        for i in range(spread.shape[0]):
            spread[i] = solved


def dense_kernel(newest, line, at, levels, blocks, store, right, table, *rest):
    m = len(levels)
    inverses, (*rest, room, sems) = rest[:m], rest[m:]
    ncol, slots = blocks.shape[0], blocks.shape[2]
    copies = run([pltpu.make_async_copy(blocks.at[c, at], room.at[c], sems.at[c]) for c in range(ncol)])
    total = jnp.zeros(store.shape[1:], F32)
    for c in range(ncol):
        copies[c].wait()
        for slot in range(slots):
            total += dot(pick([store], newest, table[c, line * slots + slot], row), room[c, slot])
    finish_row(total, right, levels[0], inverses, levels, rest)


def sparse_kernel(newest, line, at, levels, blocks, store, right, before, found, ready, *rest):
    m = len(levels)
    inverses, (*rest, room, sems) = rest[:m], rest[m:]
    ncol, slots = blocks.shape[0], blocks.shape[2]
    cap = ready.shape[0]
    n = found[ncol * slots]

    def fetch(j):
        i = found[j] // 32
        return pltpu.make_async_copy(blocks.at[i // slots, at, i % slots], room.at[j - cap], sems.at[j - cap])

    @pl.loop(cap, jnp.maximum(n, cap))
    def _(j):
        fetch(j).start()

    def some(low, high, load, k, total):
        terms = []
        for u in range(STEP):
            j = low + k * STEP + u
            to = jnp.minimum(j, high - 1)
            picked = store[found[to] % 32]
            picked = jnp.where(j < high, picked, jnp.zeros_like(picked))
            terms.append(dot(picked, load(to)))
        while len(terms) > 1:
            terms = [x + y for x, y in zip(terms[::2], terms[1::2])]
        return total + terms[0]

    held = jnp.minimum(n, cap)
    total = lax.fori_loop(
        0, (held + STEP - 1) // STEP, lambda k, total: some(0, held, lambda j: ready[j], k, total), before[...]
    )

    @pl.loop(cap, jnp.maximum(n, cap))
    def _(j):
        fetch(j).wait()

    more = jnp.maximum(n - cap, 0)
    total = lax.fori_loop(
        0, (more + STEP - 1) // STEP, lambda k, total: some(cap, n, lambda j: room[j - cap], k, total), total
    )
    finish_row(total, right, levels[0], inverses, levels, rest)


def solve(newest, line, at, levels, table, blocks, store, right, before, inverses, done=()):
    part, size = right.shape[-2:]
    ncol, slots = blocks.shape[0], blocks.shape[2]
    width = store.shape[0]
    if done:
        out_shape = jax.ShapeDtypeStruct((ncol, len(done) + 1, part, size), BF)
        out_specs = VMEM
    else:
        out_shape = [jax.ShapeDtypeStruct((part, size), BF), jax.ShapeDtypeStruct((width, part, size), BF)]
        out_specs = [VMEM, VMEM]
    if before:
        body, own, own_specs = sparse_kernel, before, [VMEM, SMEM, VMEM]
        copies = ncol * slots - before[2].shape[0]
        room = (copies, size, size)
    else:
        body, own, own_specs = dense_kernel, [table], [SMEM]
        room = (ncol, slots, size, size)
        copies = ncol
    return pl.pallas_call(
        functools.partial(body, newest, line, at, levels),
        out_shape=out_shape,
        in_specs=[ANY, VMEM, VMEM] + own_specs + [VMEM] * (len(inverses) + len(done)),
        out_specs=out_specs,
        scratch_shapes=[pltpu.VMEM(room, BF), pltpu.SemaphoreType.DMA((copies,))],
        compiler_params=params(10),
        cost_estimate=pl.CostEstimate(flops=2 * ncol * slots * part * size * size, bytes_accessed=4 << 20, transcendentals=0),
        name="solve",
    )(hbm(blocks), store, right, *own, *inverses, *done)


def shards(
    right_side,
    lower_inverse,
    upper_inverse,
    lower_blocks,
    lower_sources,
    lower_counts,
    upper_blocks,
    upper_sources,
    upper_counts,
):
    width = lax.axis_size(ROW)
    ncol = lax.axis_size(COL)
    group = width // ncol
    column = lax.axis_index(COL)
    levels, nrhs, size = right_side.shape[1:]
    slots = lower_blocks.shape[2]
    part = nrhs // ncol

    last = LAST_SPLIT
    lines = [(0, level - 1) for level in range(last + 1, levels)] + [(1, level) for level in range(levels - 2, -1, -1)]
    *rows, right, first, copies = begin(
        lines, RUNS, jnp.full((1,), column, I32), lower_blocks, upper_blocks, right_side, lower_inverse, ncol, width
    )
    gathered = []
    for count, part_rows in zip(RUNS, rows):
        whole = lax.all_gather(part_rows, COL, axis=0)
        gathered.extend((whole, i) for i in range(count))

    def places(sources, counts, by_column):
        s, n = sources[0], counts[0]
        live = jnp.arange(slots, dtype=I32)[None] < n
        g = s % width // ncol
        place = s // width * width + g
        if by_column:
            place = (s // width * ncol + s % ncol) * group + g
        return jnp.where(live, place, -1)

    own_table = places(lower_sources, lower_counts, False)
    late = jnp.concatenate(
        [
            places(lower_sources, lower_counts, True)[last:],
            places(upper_sources, upper_counts, True)[::-1],
        ]
    ).reshape(-1)
    late = jnp.pad(late.astype(F32)[None], ((0, 7), (0, size - late.shape[0])))

    def spread(copies):
        return lax.all_to_all(copies, TURNED, 0, 0, tiled=True)

    def by_column(whole):
        return lax.all_to_all(whole.reshape(ncol, group, part, size), COL, 0, 0, tiled=True)

    stores, halves, own = [spread(copies)], [], [first]
    for level in range(1, last + 1):
        halves.append(by_column(stores[-1]))
        partial = update(level - 1, own_table, lower_blocks, halves, late if level == 1 else None)
        parts = lax.all_to_all(partial, COL, 0, 0, tiled=True)
        solved, copies, *rest = finish(level, parts, right, lower_inverse, width)
        if rest:
            table = rest[0]
        own.append(solved)
        if level < last:
            stores.append(spread(copies))

    def step(ready, line, olds, first, newest, copies):
        blocks, at = gathered[line]
        copies, tied = lax.optimization_barrier((copies, table))
        before = older(READY[ready], first, line, at, newest, tied, blocks, olds) if olds else []
        return spread(copies), before

    line = 0
    for level in range(last + 1, levels):
        newest, before = step(0, line, stores, 0, level - 1, copies)
        ends = [lower_inverse], [level]
        if level == levels - 1:
            ends = [lower_inverse, upper_inverse], [level, level]
        blocks, at = gathered[line]
        solved, copies = solve(level - 1, line, at, ends[1], table, blocks, newest, right, before, ends[0])
        own.append(solved)
        stores.append(newest)
        line += 1
    result, stores = [solved], []
    for level in range(levels - 2, -1, -1):
        newest, before = step(1, line, stores, level + 2, level + 1, copies)
        blocks, at = gathered[line]
        done = result if level == 0 else ()
        solved = solve(level + 1, line, at, [level], table, blocks, newest, own[level], before, [upper_inverse], done)
        if level > 0:
            solved, copies = solved
            result.insert(0, solved)
            stores.insert(0, newest)
        line += 1
    whole = lax.all_to_all(solved, COL, 0, 0, tiled=True)
    return jnp.transpose(whole, (1, 0, 2, 3)).reshape(1, levels, nrhs, size)


def solution(mesh):
    width, ncol = mesh.devices.shape
    grid = Mesh(mesh.devices.reshape(width // ncol, ncol, ncol // 2, 2), ROW + COL)
    in_specs = (
        P(ROW, None, None, None),
        P(ROW, None, None, None),
        P(ROW, None, None, None),
        P(ROW, None, COL, None, None),
        P(ROW, None, COL),
        P(ROW, None, COL),
        P(ROW, None, COL, None, None),
        P(ROW, None, COL),
        P(ROW, None, COL),
    )
    out_specs = P(ROW, None, None, None)
    return jax.shard_map(shards, mesh=grid, in_specs=in_specs, out_specs=out_specs, check_vma=False)
```

```python
import functools

import jax
import jax.numpy as jnp
from jax import lax
from jax.experimental import pallas as pl
from jax.experimental.pallas import tpu as pltpu
from jax.sharding import Mesh
from jax.sharding import PartitionSpec as P

BF = jnp.bfloat16
F32 = jnp.float32
I32 = jnp.int32
NT = (((1,), (1,)), ((), ()))
ROW = ("g", "z")
TURNED = ("z", "g")
COL = ("x", "core")
SMEM = pl.BlockSpec(memory_space=pltpu.SMEM)
VMEM = pl.BlockSpec(memory_space=pltpu.VMEM)
ANY = pl.BlockSpec(memory_space=pl.ANY)
HBM = pl.BlockSpec(memory_space=pltpu.HBM)
LAST_SPLIT = 3
RUNS = (4, 2, 1)
STEP = 4
READY = (6, 10)


def dot(x, y):
    return lax.dot_general(x, y, NT, preferred_element_type=F32)


def run(copies):
    for copy in copies:
        copy.start()
    return copies


def params(mib):
    return pltpu.CompilerParams(vmem_limit_bytes=mib << 20)


def hbm(blocks):
    return pltpu.with_memory_space_constraint(blocks, pltpu.HBM)


def first_kernel(lines, low_blocks, high_blocks, out, room, loads, stores):
    sources = (low_blocks, high_blocks)
    reads = run(
        [pltpu.make_async_copy(sources[which].at[0, k], room.at[i], loads.at[i]) for i, (which, k) in enumerate(lines)]
    )
    writes = [pltpu.make_async_copy(room.at[i], out.at[i], stores.at[i]) for i in range(len(lines))]
    for read, write in zip(reads, writes):
        read.wait()
        write.start()
    for write in writes:
        write.wait()


def first_run(lines, low_blocks, high_blocks):
    block = low_blocks.shape[2:]
    n = len(lines)
    return pl.pallas_call(
        functools.partial(first_kernel, lines),
        out_shape=pltpu.HBM((n,) + block, BF),
        in_specs=[ANY] * 2,
        out_specs=ANY,
        scratch_shapes=[
            pltpu.VMEM((n,) + block, BF),
            pltpu.SemaphoreType.DMA((n,)),
            pltpu.SemaphoreType.DMA((n,)),
        ],
        compiler_params=params(10),
        name="first",
    )(hbm(low_blocks), hbm(high_blocks))


def begin_kernel(lines, runs, column, low_blocks, high_blocks, right_side, inverse, *rest):
    outs, rest = rest[: len(runs)], rest[len(runs) :]
    right, out, spread, diag, room, loads, stores, sems = rest
    part = right.shape[1]
    start = pl.multiple_of(column[0] * part, part)
    small = run(
        [
            pltpu.make_async_copy(right_side.at[0, :, pl.ds(start, part)], right, sems.at[0]),
            pltpu.make_async_copy(inverse.at[0, 0], diag, sems.at[1]),
        ]
    )
    sources = (low_blocks, high_blocks)
    reads = run(
        [pltpu.make_async_copy(sources[which].at[0, k], room.at[i], loads.at[i]) for i, (which, k) in enumerate(lines)]
    )
    places = [(j, i) for j, count in enumerate(runs) for i in range(count)]
    writes = [pltpu.make_async_copy(room.at[n], outs[j].at[i], stores.at[n]) for n, (j, i) in enumerate(places)]
    for copy in small:
        copy.wait()
    solved = dot(right[0], diag[...]).astype(BF)
    out[...] = solved
    for i in range(spread.shape[0]):
        spread[i] = solved
    for read, write in zip(reads, writes):
        read.wait()
        write.start()
    for write in writes:
        write.wait()


def begin(lines, runs, column, low_blocks, high_blocks, right_side, inverse, ncol, width):
    block = low_blocks.shape[2:]
    levels, nrhs, size = right_side.shape[1:]
    part = nrhs // ncol
    n = len(lines)
    return pl.pallas_call(
        functools.partial(begin_kernel, lines, runs),
        out_shape=[pltpu.HBM((count,) + block, BF) for count in runs]
        + [jax.ShapeDtypeStruct(shape, BF) for shape in ((levels, part, size), (part, size), (width, part, size))],
        in_specs=[SMEM] + [ANY] * 4,
        out_specs=[ANY] * len(runs) + [VMEM] * 3,
        scratch_shapes=[
            pltpu.VMEM((size, size), BF),
            pltpu.VMEM((n,) + block, BF),
            pltpu.SemaphoreType.DMA((n,)),
            pltpu.SemaphoreType.DMA((n,)),
            pltpu.SemaphoreType.DMA((2,)),
        ],
        compiler_params=params(10),
        name="begin",
    )(column, hbm(low_blocks), hbm(high_blocks), hbm(right_side), hbm(inverse))


def pick(stores, first, place, load):
    width = 32
    at = jnp.maximum(place, 0)
    level, index = at // width - first, at % width
    picked = load(stores[0], index)
    for i in range(1, len(stores)):
        picked = jnp.where(level == i, load(stores[i], index), picked)
    live = (place >= first * width) & (place < (first + len(stores)) * width)
    return jnp.where(live, picked, jnp.zeros_like(picked))


def update_kernel(level, n, extra, table, blocks, *rest):
    stores, rest = rest[:n], rest[n:]
    out = rest[-1]
    ncol, group, part, size = stores[0].shape

    def load(store, index):
        return store[:, index % group].reshape(ncol * part, size)

    total = jnp.zeros((ncol * part, size), F32)
    for slot in range(blocks.shape[2]):
        total += dot(pick(stores, 0, table[level, slot], load), blocks[0, level, slot])
    out[:, :part] = total.reshape(ncol, part, size)
    if extra:
        out[:, part:] = jnp.broadcast_to(rest[0][...][None], (ncol, extra, size))


def update(level, table, blocks, stores, late=None):
    slots, size = blocks.shape[2], blocks.shape[3]
    ncol, group, part, _ = stores[0].shape
    n = len(stores)
    extra = 0 if late is None else late.shape[0]
    return pl.pallas_call(
        functools.partial(update_kernel, level, n, extra),
        out_shape=jax.ShapeDtypeStruct((ncol, part + extra, size), F32),
        in_specs=[SMEM, VMEM] + [VMEM] * (n + (late is not None)),
        out_specs=VMEM,
        compiler_params=params(4),
        cost_estimate=pl.CostEstimate(flops=2 * slots * ncol * part * size * size, bytes_accessed=1 << 20, transcendentals=0),
        name="update",
    )(table, blocks, *stores, *([] if late is None else [late]))


def finish_kernel(level, parts, right, inverse, out, spread, *table):
    residual = right[level]
    part = residual.shape[0]
    if parts is not None:
        total = parts[0, :part]
        for i in range(1, parts.shape[0]):
            total = total + parts[i, :part]
        residual = (residual.astype(F32) - total).astype(BF)
    solved = dot(residual, inverse[0, level]).astype(BF)
    out[...] = solved
    for i in range(spread.shape[0]):
        spread[i] = solved
    if table:
        for i in range(parts.shape[0]):
            table[0][i : i + 1] = parts[i, part : part + 1, :128].astype(I32)


def finish(level, parts, right, inverse, width):
    part, size = right.shape[1:]
    body = functools.partial(finish_kernel, level)
    out_shape = [jax.ShapeDtypeStruct((part, size), BF), jax.ShapeDtypeStruct((width, part, size), BF)]
    if parts is None:
        body = functools.partial(finish_kernel, level, None)
    elif parts.shape[1] > part:
        out_shape.append(jax.ShapeDtypeStruct((parts.shape[0], 128), I32))
    return pl.pallas_call(
        body,
        out_shape=out_shape,
        in_specs=([] if parts is None else [VMEM]) + [VMEM, VMEM],
        out_specs=[VMEM] * len(out_shape),
        compiler_params=params(4),
        cost_estimate=pl.CostEstimate(flops=2 * part * size * size, bytes_accessed=1 << 19, transcendentals=0),
        name="finish",
    )(*([] if parts is None else [parts]), right, inverse)


def row(store, index):
    return store[index]


def older_kernel(first, line, at, newest, table, blocks, *rest):
    *stores, out, found, ready, room, sems, ready_sems = rest
    ncol, slots = room.shape[:2]
    cap = ready.shape[0]
    copies = run([pltpu.make_async_copy(blocks.at[c, at], room.at[c], sems.at[c]) for c in range(ncol)])
    n = jnp.int32(0)
    for i in range(ncol * slots):
        place = table[i // slots, line * slots + i % slots]
        hit = (place >= newest * 32) & (place < newest * 32 + 32)

        @pl.when(hit)
        def _():
            found[n] = i * 32 + place - newest * 32

        @pl.when(hit & (n < cap))
        def _():
            pltpu.make_async_copy(blocks.at[i // slots, at, i % slots], ready.at[n], ready_sems.at[n]).start()

        n = n + jnp.where(hit, 1, 0)
    found[ncol * slots] = n
    total = jnp.zeros(out.shape, F32)
    for c in range(ncol):
        copies[c].wait()
        for slot in range(slots):
            total += dot(pick(stores, first, table[c, line * slots + slot], row), room[c, slot])
    out[...] = total

    @pl.loop(0, jnp.minimum(n, cap))
    def _(j):
        pltpu.make_async_copy(blocks.at[0, at, 0], ready.at[j], ready_sems.at[j]).wait()


def older(ready, first, line, at, newest, table, blocks, stores):
    ncol, _, slots, size, _ = blocks.shape
    part = stores[0].shape[1]
    return pl.pallas_call(
        functools.partial(older_kernel, first, line, at, newest),
        out_shape=[
            pltpu.VMEM((part, size), F32),
            jax.ShapeDtypeStruct((64,), I32),
            pltpu.VMEM((ready, size, size), BF),
        ],
        in_specs=[SMEM, ANY] + [VMEM] * len(stores),
        out_specs=[VMEM, SMEM, VMEM],
        scratch_shapes=[
            pltpu.VMEM((ncol, slots, size, size), BF),
            pltpu.SemaphoreType.DMA((ncol,)),
            pltpu.SemaphoreType.DMA((ready,)),
        ],
        compiler_params=params(10),
        cost_estimate=pl.CostEstimate(flops=2 * ncol * slots * part * size * size, bytes_accessed=13 << 20, transcendentals=0),
        name="older",
    )(table, hbm(blocks), *stores)


def finish_row(total, right, level, inverses, levels, rest):
    solved = ((right[level] if len(right.shape) > 2 else right[...]).astype(F32) - total).astype(BF)
    for i, level in enumerate(levels):
        solved = dot(solved, inverses[i][0, level]).astype(BF)
    if len(rest) > 2:
        *done, out = rest
        for i in range(out.shape[0]):
            out[i, 0] = solved
            for j, ref in enumerate(done):
                out[i, j + 1] = ref[...]
    else:
        out, spread = rest
        out[...] = solved
        for i in range(spread.shape[0]):
            spread[i] = solved


def dense_kernel(newest, line, at, levels, blocks, store, right, table, *rest):
    m = len(levels)
    inverses, (*rest, room, sems) = rest[:m], rest[m:]
    ncol, slots = blocks.shape[0], blocks.shape[2]
    copies = run([pltpu.make_async_copy(blocks.at[c, at], room.at[c], sems.at[c]) for c in range(ncol)])
    total = jnp.zeros(store.shape[1:], F32)
    for c in range(ncol):
        copies[c].wait()
        for slot in range(slots):
            total += dot(pick([store], newest, table[c, line * slots + slot], row), room[c, slot])
    finish_row(total, right, levels[0], inverses, levels, rest)


def sparse_kernel(newest, line, at, levels, blocks, store, right, before, found, ready, *rest):
    m = len(levels)
    inverses, (*rest, room, sems) = rest[:m], rest[m:]
    ncol, slots = blocks.shape[0], blocks.shape[2]
    cap = ready.shape[0]
    n = found[ncol * slots]

    def fetch(j):
        i = found[j] // 32
        return pltpu.make_async_copy(blocks.at[i // slots, at, i % slots], room.at[j - cap], sems.at[j - cap])

    @pl.loop(cap, jnp.maximum(n, cap))
    def _(j):
        fetch(j).start()

    def some(low, high, load, k, total):
        terms = []
        for u in range(STEP):
            j = low + k * STEP + u
            to = jnp.minimum(j, high - 1)
            picked = store[found[to] % 32]
            picked = jnp.where(j < high, picked, jnp.zeros_like(picked))
            terms.append(dot(picked, load(to)))
        while len(terms) > 1:
            terms = [x + y for x, y in zip(terms[::2], terms[1::2])]
        return total + terms[0]

    held = jnp.minimum(n, cap)
    total = lax.fori_loop(
        0, (held + STEP - 1) // STEP, lambda k, total: some(0, held, lambda j: ready[j], k, total), before[...]
    )

    @pl.loop(cap, jnp.maximum(n, cap))
    def _(j):
        fetch(j).wait()

    more = jnp.maximum(n - cap, 0)
    total = lax.fori_loop(
        0, (more + STEP - 1) // STEP, lambda k, total: some(cap, n, lambda j: room[j - cap], k, total), total
    )
    finish_row(total, right, levels[0], inverses, levels, rest)


def solve(newest, line, at, levels, table, blocks, store, right, before, inverses, done=()):
    part, size = right.shape[-2:]
    ncol, slots = blocks.shape[0], blocks.shape[2]
    width = store.shape[0]
    if done:
        out_shape = jax.ShapeDtypeStruct((ncol, len(done) + 1, part, size), BF)
        out_specs = VMEM
    else:
        out_shape = [jax.ShapeDtypeStruct((part, size), BF), jax.ShapeDtypeStruct((width, part, size), BF)]
        out_specs = [VMEM, VMEM]
    if before:
        body, own, own_specs = sparse_kernel, before, [VMEM, SMEM, VMEM]
        copies = ncol * slots - before[2].shape[0]
        room = (copies, size, size)
    else:
        body, own, own_specs = dense_kernel, [table], [SMEM]
        room = (ncol, slots, size, size)
        copies = ncol
    return pl.pallas_call(
        functools.partial(body, newest, line, at, levels),
        out_shape=out_shape,
        in_specs=[ANY, VMEM, VMEM] + own_specs + [VMEM] * (len(inverses) + len(done)),
        out_specs=out_specs,
        scratch_shapes=[pltpu.VMEM(room, BF), pltpu.SemaphoreType.DMA((copies,))],
        compiler_params=params(10),
        cost_estimate=pl.CostEstimate(flops=2 * ncol * slots * part * size * size, bytes_accessed=4 << 20, transcendentals=0),
        name="solve",
    )(hbm(blocks), store, right, *own, *inverses, *done)


def shards(
    right_side,
    lower_inverse,
    upper_inverse,
    lower_blocks,
    lower_sources,
    lower_counts,
    upper_blocks,
    upper_sources,
    upper_counts,
):
    width = lax.axis_size(ROW)
    ncol = lax.axis_size(COL)
    group = width // ncol
    column = lax.axis_index(COL)
    levels, nrhs, size = right_side.shape[1:]
    slots = lower_blocks.shape[2]
    part = nrhs // ncol

    last = LAST_SPLIT
    lines = [(0, level - 1) for level in range(last + 1, levels)] + [(1, level) for level in range(levels - 2, -1, -1)]
    head = first_run(lines[: RUNS[0]], lower_blocks, upper_blocks)
    *rows, right, first, copies = begin(
        lines[RUNS[0] :],
        RUNS[1:],
        jnp.full((1,), column, I32),
        lower_blocks,
        upper_blocks,
        right_side,
        lower_inverse,
        ncol,
        width,
    )
    gathered = []
    for count, part_rows in zip(RUNS, [head] + rows):
        whole = lax.all_gather(part_rows, COL, axis=0)
        gathered.extend((whole, i) for i in range(count))

    def places(sources, counts, by_column):
        s, n = sources[0], counts[0]
        live = jnp.arange(slots, dtype=I32)[None] < n
        g = s % width // ncol
        place = s // width * width + g
        if by_column:
            place = (s // width * ncol + s % ncol) * group + g
        return jnp.where(live, place, -1)

    own_table = places(lower_sources, lower_counts, False)
    late = jnp.concatenate(
        [
            places(lower_sources, lower_counts, True)[last:],
            places(upper_sources, upper_counts, True)[::-1],
        ]
    ).reshape(-1)
    late = jnp.pad(late.astype(F32)[None], ((0, 7), (0, size - late.shape[0])))

    def spread(copies):
        return lax.all_to_all(copies, TURNED, 0, 0, tiled=True)

    def by_column(whole):
        return lax.all_to_all(whole.reshape(ncol, group, part, size), COL, 0, 0, tiled=True)

    stores, halves, own = [spread(copies)], [], [first]
    for level in range(1, last + 1):
        halves.append(by_column(stores[-1]))
        partial = update(level - 1, own_table, lower_blocks, halves, late if level == 1 else None)
        parts = lax.all_to_all(partial, COL, 0, 0, tiled=True)
        solved, copies, *rest = finish(level, parts, right, lower_inverse, width)
        if rest:
            table = rest[0]
        own.append(solved)
        if level < last:
            stores.append(spread(copies))

    def step(ready, line, olds, first, newest, copies):
        blocks, at = gathered[line]
        copies, tied = lax.optimization_barrier((copies, table))
        before = older(READY[ready], first, line, at, newest, tied, blocks, olds) if olds else []
        return spread(copies), before

    line = 0
    for level in range(last + 1, levels):
        newest, before = step(0, line, stores, 0, level - 1, copies)
        ends = [lower_inverse], [level]
        if level == levels - 1:
            ends = [lower_inverse, upper_inverse], [level, level]
        blocks, at = gathered[line]
        solved, copies = solve(level - 1, line, at, ends[1], table, blocks, newest, right, before, ends[0])
        own.append(solved)
        stores.append(newest)
        line += 1
    result, stores = [solved], []
    for level in range(levels - 2, -1, -1):
        newest, before = step(1, line, stores, level + 2, level + 1, copies)
        blocks, at = gathered[line]
        done = result if level == 0 else ()
        solved = solve(level + 1, line, at, [level], table, blocks, newest, own[level], before, [upper_inverse], done)
        if level > 0:
            solved, copies = solved
            result.insert(0, solved)
            stores.insert(0, newest)
        line += 1
    whole = lax.all_to_all(solved, COL, 0, 0, tiled=True)
    return jnp.transpose(whole, (1, 0, 2, 3)).reshape(1, levels, nrhs, size)


def solution(mesh):
    width, ncol = mesh.devices.shape
    grid = Mesh(mesh.devices.reshape(width // ncol, ncol, ncol // 2, 2), ROW + COL)
    in_specs = (
        P(ROW, None, None, None),
        P(ROW, None, None, None),
        P(ROW, None, None, None),
        P(ROW, None, COL, None, None),
        P(ROW, None, COL),
        P(ROW, None, COL),
        P(ROW, None, COL, None, None),
        P(ROW, None, COL),
        P(ROW, None, COL),
    )
    out_specs = P(ROW, None, None, None)
    return jax.shard_map(shards, mesh=grid, in_specs=in_specs, out_specs=out_specs, check_vma=False)
```

```python
import functools

import jax
import jax.numpy as jnp
from jax import lax
from jax.experimental import pallas as pl
from jax.experimental.pallas import tpu as pltpu
from jax.sharding import Mesh
from jax.sharding import PartitionSpec as P

BF = jnp.bfloat16
F32 = jnp.float32
I32 = jnp.int32
NT = (((1,), (1,)), ((), ()))
ROW = ("g", "z")
TURNED = ("z", "g")
COL = ("x", "core")
SMEM = pl.BlockSpec(memory_space=pltpu.SMEM)
VMEM = pl.BlockSpec(memory_space=pltpu.VMEM)
ANY = pl.BlockSpec(memory_space=pl.ANY)
HBM = pl.BlockSpec(memory_space=pltpu.HBM)
LAST_SPLIT = 3
RUNS = (4, 2, 1)
STEP = 4
READY = (12, 12, 20, 20, 16, 14, 10)


def dot(x, y):
    return lax.dot_general(x, y, NT, preferred_element_type=F32)


def run(copies):
    for copy in copies:
        copy.start()
    return copies


def params(mib):
    return pltpu.CompilerParams(vmem_limit_bytes=mib << 20)


def hbm(blocks):
    return pltpu.with_memory_space_constraint(blocks, pltpu.HBM)


def first_kernel(lines, low_blocks, high_blocks, out, room, loads, stores):
    sources = (low_blocks, high_blocks)
    reads = run(
        [pltpu.make_async_copy(sources[which].at[0, k], room.at[i], loads.at[i]) for i, (which, k) in enumerate(lines)]
    )
    writes = [pltpu.make_async_copy(room.at[i], out.at[i], stores.at[i]) for i in range(len(lines))]
    for read, write in zip(reads, writes):
        read.wait()
        write.start()
    for write in writes:
        write.wait()


def first_run(lines, low_blocks, high_blocks):
    block = low_blocks.shape[2:]
    n = len(lines)
    return pl.pallas_call(
        functools.partial(first_kernel, lines),
        out_shape=pltpu.HBM((n,) + block, BF),
        in_specs=[ANY] * 2,
        out_specs=ANY,
        scratch_shapes=[
            pltpu.VMEM((n,) + block, BF),
            pltpu.SemaphoreType.DMA((n,)),
            pltpu.SemaphoreType.DMA((n,)),
        ],
        compiler_params=params(10),
        name="first",
    )(hbm(low_blocks), hbm(high_blocks))


def begin_kernel(lines, runs, column, low_blocks, high_blocks, right_side, inverse, *rest):
    outs, rest = rest[: len(runs)], rest[len(runs) :]
    right, out, spread, diag, room, loads, stores, sems = rest
    part = right.shape[1]
    start = pl.multiple_of(column[0] * part, part)
    small = run(
        [
            pltpu.make_async_copy(right_side.at[0, :, pl.ds(start, part)], right, sems.at[0]),
            pltpu.make_async_copy(inverse.at[0, 0], diag, sems.at[1]),
        ]
    )
    sources = (low_blocks, high_blocks)
    reads = run(
        [pltpu.make_async_copy(sources[which].at[0, k], room.at[i], loads.at[i]) for i, (which, k) in enumerate(lines)]
    )
    places = [(j, i) for j, count in enumerate(runs) for i in range(count)]
    writes = [pltpu.make_async_copy(room.at[n], outs[j].at[i], stores.at[n]) for n, (j, i) in enumerate(places)]
    for copy in small:
        copy.wait()
    solved = dot(right[0], diag[...]).astype(BF)
    out[...] = solved
    for i in range(spread.shape[0]):
        spread[i] = solved
    for read, write in zip(reads, writes):
        read.wait()
        write.start()
    for write in writes:
        write.wait()


def begin(lines, runs, column, low_blocks, high_blocks, right_side, inverse, ncol, width):
    block = low_blocks.shape[2:]
    levels, nrhs, size = right_side.shape[1:]
    part = nrhs // ncol
    n = len(lines)
    return pl.pallas_call(
        functools.partial(begin_kernel, lines, runs),
        out_shape=[pltpu.HBM((count,) + block, BF) for count in runs]
        + [jax.ShapeDtypeStruct(shape, BF) for shape in ((levels, part, size), (part, size), (width, part, size))],
        in_specs=[SMEM] + [ANY] * 4,
        out_specs=[ANY] * len(runs) + [VMEM] * 3,
        scratch_shapes=[
            pltpu.VMEM((size, size), BF),
            pltpu.VMEM((n,) + block, BF),
            pltpu.SemaphoreType.DMA((n,)),
            pltpu.SemaphoreType.DMA((n,)),
            pltpu.SemaphoreType.DMA((2,)),
        ],
        compiler_params=params(10),
        name="begin",
    )(column, hbm(low_blocks), hbm(high_blocks), hbm(right_side), hbm(inverse))


def pick(stores, first, place, load):
    width = 32
    at = jnp.maximum(place, 0)
    level, index = at // width - first, at % width
    picked = load(stores[0], index)
    for i in range(1, len(stores)):
        picked = jnp.where(level == i, load(stores[i], index), picked)
    live = (place >= first * width) & (place < (first + len(stores)) * width)
    return jnp.where(live, picked, jnp.zeros_like(picked))


def update_kernel(level, n, extra, table, blocks, *rest):
    stores, rest = rest[:n], rest[n:]
    out = rest[-1]
    ncol, group, part, size = stores[0].shape

    def load(store, index):
        return store[:, index % group].reshape(ncol * part, size)

    total = jnp.zeros((ncol * part, size), F32)
    for slot in range(blocks.shape[2]):
        total += dot(pick(stores, 0, table[level, slot], load), blocks[0, level, slot])
    out[:, :part] = total.reshape(ncol, part, size)
    if extra:
        out[:, part:] = jnp.broadcast_to(rest[0][...][None], (ncol, extra, size))


def update(level, table, blocks, stores, late=None):
    slots, size = blocks.shape[2], blocks.shape[3]
    ncol, group, part, _ = stores[0].shape
    n = len(stores)
    extra = 0 if late is None else late.shape[0]
    return pl.pallas_call(
        functools.partial(update_kernel, level, n, extra),
        out_shape=jax.ShapeDtypeStruct((ncol, part + extra, size), F32),
        in_specs=[SMEM, VMEM] + [VMEM] * (n + (late is not None)),
        out_specs=VMEM,
        compiler_params=params(4),
        cost_estimate=pl.CostEstimate(flops=2 * slots * ncol * part * size * size, bytes_accessed=1 << 20, transcendentals=0),
        name="update",
    )(table, blocks, *stores, *([] if late is None else [late]))


def finish_kernel(level, parts, right, inverse, out, spread, *table):
    residual = right[level]
    part = residual.shape[0]
    if parts is not None:
        total = parts[0, :part]
        for i in range(1, parts.shape[0]):
            total = total + parts[i, :part]
        residual = (residual.astype(F32) - total).astype(BF)
    solved = dot(residual, inverse[0, level]).astype(BF)
    out[...] = solved
    for i in range(spread.shape[0]):
        spread[i] = solved
    if table:
        for i in range(parts.shape[0]):
            table[0][i : i + 1] = parts[i, part : part + 1, :128].astype(I32)


def finish(level, parts, right, inverse, width):
    part, size = right.shape[1:]
    body = functools.partial(finish_kernel, level)
    out_shape = [jax.ShapeDtypeStruct((part, size), BF), jax.ShapeDtypeStruct((width, part, size), BF)]
    if parts is None:
        body = functools.partial(finish_kernel, level, None)
    elif parts.shape[1] > part:
        out_shape.append(jax.ShapeDtypeStruct((parts.shape[0], 128), I32))
    return pl.pallas_call(
        body,
        out_shape=out_shape,
        in_specs=([] if parts is None else [VMEM]) + [VMEM, VMEM],
        out_specs=[VMEM] * len(out_shape),
        compiler_params=params(4),
        cost_estimate=pl.CostEstimate(flops=2 * part * size * size, bytes_accessed=1 << 19, transcendentals=0),
        name="finish",
    )(*([] if parts is None else [parts]), right, inverse)


def row(store, index):
    return store[index]


def older_kernel(first, line, at, newest, table, blocks, *rest):
    *stores, out, found, ready, room, sems, ready_sems = rest
    ncol, slots = blocks.shape[0], blocks.shape[2]
    cap = ready.shape[0]
    copies = []
    if stores:
        copies = run([pltpu.make_async_copy(blocks.at[c, at], room.at[c], sems.at[c]) for c in range(ncol)])
    n = jnp.int32(0)
    for i in range(ncol * slots):
        place = table[i // slots, line * slots + i % slots]
        hit = (place >= newest * 32) & (place < newest * 32 + 32)

        @pl.when(hit)
        def _():
            found[n] = i * 32 + place - newest * 32

        @pl.when(hit & (n < cap))
        def _():
            pltpu.make_async_copy(blocks.at[i // slots, at, i % slots], ready.at[n], ready_sems.at[n]).start()

        n = n + jnp.where(hit, 1, 0)
    found[ncol * slots] = n
    total = jnp.zeros(out.shape, F32)
    for c, copy in enumerate(copies):
        copy.wait()
        for slot in range(slots):
            total += dot(pick(stores, first, table[c, line * slots + slot], row), room[c, slot])
    out[...] = total

    @pl.loop(0, jnp.minimum(n, cap))
    def _(j):
        pltpu.make_async_copy(blocks.at[0, at, 0], ready.at[j], ready_sems.at[j]).wait()


def older(ready, first, line, at, newest, table, blocks, stores, part):
    ncol, _, slots, size, _ = blocks.shape
    return pl.pallas_call(
        functools.partial(older_kernel, first, line, at, newest),
        out_shape=[
            pltpu.VMEM((part, size), F32),
            jax.ShapeDtypeStruct((64,), I32),
            pltpu.VMEM((ready, size, size), BF),
        ],
        in_specs=[SMEM, ANY] + [VMEM] * len(stores),
        out_specs=[VMEM, SMEM, VMEM],
        scratch_shapes=[
            pltpu.VMEM((ncol if stores else 1, slots, size, size), BF),
            pltpu.SemaphoreType.DMA((ncol,)),
            pltpu.SemaphoreType.DMA((ready,)),
        ],
        compiler_params=params(10),
        cost_estimate=pl.CostEstimate(flops=2 * ncol * slots * part * size * size, bytes_accessed=13 << 20, transcendentals=0),
        name="older",
    )(table, hbm(blocks), *stores)


def fetch_ends(inverses, levels, diag, sems):
    return run(
        [
            pltpu.make_async_copy(ref.at[0, level], diag.at[i], sems.at[i])
            for i, (ref, level) in enumerate(zip(inverses, levels))
        ]
    )


def finish_row(total, right, level, ends, diag, rest):
    solved = ((right[level] if len(right.shape) > 2 else right[...]).astype(F32) - total).astype(BF)
    for i, end in enumerate(ends):
        end.wait()
        solved = dot(solved, diag[i]).astype(BF)
    if len(rest) > 2:
        *done, out = rest
        for i in range(out.shape[0]):
            out[i, 0] = solved
            for j, ref in enumerate(done):
                out[i, j + 1] = ref[...]
    else:
        out, spread = rest
        out[...] = solved
        for i in range(spread.shape[0]):
            spread[i] = solved


def sparse_kernel(newest, line, at, levels, blocks, store, right, before, found, ready, *rest):
    m = len(levels)
    inverses, (*rest, diag, room, sems, end_sems) = rest[:m], rest[m:]
    ncol, slots = blocks.shape[0], blocks.shape[2]
    cap = ready.shape[0]
    n = found[ncol * slots]
    ends = fetch_ends(inverses, levels, diag, end_sems)

    def fetch(j):
        i = found[j] // 32
        return pltpu.make_async_copy(blocks.at[i // slots, at, i % slots], room.at[j - cap], sems.at[j - cap])

    @pl.loop(cap, jnp.maximum(n, cap))
    def _(j):
        fetch(j).start()

    def some(low, high, load, k, total):
        terms = []
        for u in range(STEP):
            j = low + k * STEP + u
            to = jnp.minimum(j, high - 1)
            picked = store[found[to] % 32]
            picked = jnp.where(j < high, picked, jnp.zeros_like(picked))
            terms.append(dot(picked, load(to)))
        while len(terms) > 1:
            terms = [x + y for x, y in zip(terms[::2], terms[1::2])]
        return total + terms[0]

    held = jnp.minimum(n, cap)
    total = lax.fori_loop(
        0, (held + STEP - 1) // STEP, lambda k, total: some(0, held, lambda j: ready[j], k, total), before[...]
    )

    @pl.loop(cap, jnp.maximum(n, cap))
    def _(j):
        fetch(j).wait()

    more = jnp.maximum(n - cap, 0)
    total = lax.fori_loop(
        0, (more + STEP - 1) // STEP, lambda k, total: some(cap, n, lambda j: room[j - cap], k, total), total
    )
    finish_row(total, right, levels[0], ends, diag, rest)


def solve(newest, line, at, levels, table, blocks, store, right, before, inverses, done=()):
    part, size = right.shape[-2:]
    ncol, slots = blocks.shape[0], blocks.shape[2]
    width = store.shape[0]
    if done:
        out_shape = jax.ShapeDtypeStruct((ncol, len(done) + 1, part, size), BF)
        out_specs = VMEM
    else:
        out_shape = [jax.ShapeDtypeStruct((part, size), BF), jax.ShapeDtypeStruct((width, part, size), BF)]
        out_specs = [VMEM, VMEM]
    copies = ncol * slots - before[2].shape[0]
    return pl.pallas_call(
        functools.partial(sparse_kernel, newest, line, at, levels),
        out_shape=out_shape,
        in_specs=[ANY, VMEM, VMEM, VMEM, SMEM, VMEM] + [ANY] * len(inverses) + [VMEM] * len(done),
        out_specs=out_specs,
        scratch_shapes=[
            pltpu.VMEM((len(inverses), size, size), BF),
            pltpu.VMEM((copies, size, size), BF),
            pltpu.SemaphoreType.DMA((copies,)),
            pltpu.SemaphoreType.DMA((len(inverses),)),
        ],
        compiler_params=params(10),
        cost_estimate=pl.CostEstimate(flops=2 * ncol * slots * part * size * size, bytes_accessed=4 << 20, transcendentals=0),
        name="solve",
    )(hbm(blocks), store, right, *before, *[hbm(ref) for ref in inverses], *done)


def shards(
    right_side,
    lower_inverse,
    upper_inverse,
    lower_blocks,
    lower_sources,
    lower_counts,
    upper_blocks,
    upper_sources,
    upper_counts,
):
    width = lax.axis_size(ROW)
    ncol = lax.axis_size(COL)
    group = width // ncol
    column = lax.axis_index(COL)
    levels, nrhs, size = right_side.shape[1:]
    slots = lower_blocks.shape[2]
    part = nrhs // ncol

    last = LAST_SPLIT
    lines = [(0, level - 1) for level in range(last + 1, levels)] + [(1, level) for level in range(levels - 2, -1, -1)]
    head = first_run(lines[: RUNS[0]], lower_blocks, upper_blocks)
    *rows, right, first, copies = begin(
        lines[RUNS[0] :],
        RUNS[1:],
        jnp.full((1,), column, I32),
        lower_blocks,
        upper_blocks,
        right_side,
        lower_inverse,
        ncol,
        width,
    )
    gathered = []
    for count, part_rows in zip(RUNS, [head] + rows):
        whole = lax.all_gather(part_rows, COL, axis=0)
        gathered.extend((whole, i) for i in range(count))

    def places(sources, counts, by_column):
        s, n = sources[0], counts[0]
        live = jnp.arange(slots, dtype=I32)[None] < n
        g = s % width // ncol
        place = s // width * width + g
        if by_column:
            place = (s // width * ncol + s % ncol) * group + g
        return jnp.where(live, place, -1)

    own_table = places(lower_sources, lower_counts, False)
    late = jnp.concatenate(
        [
            places(lower_sources, lower_counts, True)[last:],
            places(upper_sources, upper_counts, True)[::-1],
        ]
    ).reshape(-1)
    late = jnp.pad(late.astype(F32)[None], ((0, 7), (0, size - late.shape[0])))

    def spread(copies):
        return lax.all_to_all(copies, TURNED, 0, 0, tiled=True)

    def by_column(whole):
        return lax.all_to_all(whole.reshape(ncol, group, part, size), COL, 0, 0, tiled=True)

    stores, halves, own = [spread(copies)], [], [first]
    for level in range(1, last + 1):
        halves.append(by_column(stores[-1]))
        partial = update(level - 1, own_table, lower_blocks, halves, late if level == 1 else None)
        parts = lax.all_to_all(partial, COL, 0, 0, tiled=True)
        solved, copies, *rest = finish(level, parts, right, lower_inverse, width)
        if rest:
            table = rest[0]
        own.append(solved)
        if level < last:
            stores.append(spread(copies))

    def step(line, olds, first, newest, copies):
        blocks, at = gathered[line]
        copies, tied = lax.optimization_barrier((copies, table))
        before = older(READY[line], first, line, at, newest, tied, blocks, olds, part)
        return spread(copies), before

    line = 0
    for level in range(last + 1, levels):
        newest, before = step(line, stores, 0, level - 1, copies)
        ends = [lower_inverse], [level]
        if level == levels - 1:
            ends = [lower_inverse, upper_inverse], [level, level]
        blocks, at = gathered[line]
        solved, copies = solve(level - 1, line, at, ends[1], table, blocks, newest, right, before, ends[0])
        own.append(solved)
        stores.append(newest)
        line += 1
    result, stores = [solved], []
    for level in range(levels - 2, -1, -1):
        newest, before = step(line, stores, level + 2, level + 1, copies)
        blocks, at = gathered[line]
        done = result if level == 0 else ()
        solved = solve(level + 1, line, at, [level], table, blocks, newest, own[level], before, [upper_inverse], done)
        if level > 0:
            solved, copies = solved
            result.insert(0, solved)
            stores.insert(0, newest)
        line += 1
    whole = lax.all_to_all(solved, COL, 0, 0, tiled=True)
    return jnp.transpose(whole, (1, 0, 2, 3)).reshape(1, levels, nrhs, size)


def solution(mesh):
    width, ncol = mesh.devices.shape
    grid = Mesh(mesh.devices.reshape(width // ncol, ncol, ncol // 2, 2), ROW + COL)
    in_specs = (
        P(ROW, None, None, None),
        P(ROW, None, None, None),
        P(ROW, None, None, None),
        P(ROW, None, COL, None, None),
        P(ROW, None, COL),
        P(ROW, None, COL),
        P(ROW, None, COL, None, None),
        P(ROW, None, COL),
        P(ROW, None, COL),
    )
    out_specs = P(ROW, None, None, None)
    return jax.shard_map(shards, mesh=grid, in_specs=in_specs, out_specs=out_specs, check_vma=False)
```

```python
import functools

import jax
import jax.numpy as jnp
from jax import lax
from jax.experimental import pallas as pl
from jax.experimental.pallas import tpu as pltpu
from jax.sharding import Mesh
from jax.sharding import PartitionSpec as P

BF = jnp.bfloat16
F32 = jnp.float32
I32 = jnp.int32
NT = (((1,), (1,)), ((), ()))
ROW = ("g", "z")
TURNED = ("z", "g")
COL = ("x", "core")
SMEM = pl.BlockSpec(memory_space=pltpu.SMEM)
VMEM = pl.BlockSpec(memory_space=pltpu.VMEM)
ANY = pl.BlockSpec(memory_space=pl.ANY)
HBM = pl.BlockSpec(memory_space=pltpu.HBM)
LAST_SPLIT = 3
RUNS = (4, 2, 1)
STEP = 4
READY = (12, 12, 20, 20, 16, 14, 10)


def dot(x, y):
    return lax.dot_general(x, y, NT, preferred_element_type=F32)


def run(copies):
    for copy in copies:
        copy.start()
    return copies


def params(mib):
    return pltpu.CompilerParams(vmem_limit_bytes=mib << 20)


def hbm(blocks):
    return pltpu.with_memory_space_constraint(blocks, pltpu.HBM)


def first_kernel(lines, low_blocks, high_blocks, out, room, loads, stores):
    sources = (low_blocks, high_blocks)
    reads = run(
        [pltpu.make_async_copy(sources[which].at[0, k], room.at[i], loads.at[i]) for i, (which, k) in enumerate(lines)]
    )
    writes = [pltpu.make_async_copy(room.at[i], out.at[i], stores.at[i]) for i in range(len(lines))]
    for read, write in zip(reads, writes):
        read.wait()
        write.start()
    for write in writes:
        write.wait()


def first_run(lines, low_blocks, high_blocks):
    block = low_blocks.shape[2:]
    n = len(lines)
    return pl.pallas_call(
        functools.partial(first_kernel, lines),
        out_shape=pltpu.HBM((n,) + block, BF),
        in_specs=[ANY] * 2,
        out_specs=ANY,
        scratch_shapes=[
            pltpu.VMEM((n,) + block, BF),
            pltpu.SemaphoreType.DMA((n,)),
            pltpu.SemaphoreType.DMA((n,)),
        ],
        compiler_params=params(10),
        name="first",
    )(hbm(low_blocks), hbm(high_blocks))


def begin_kernel(lines, runs, column, low_blocks, high_blocks, right_side, inverse, *rest):
    outs, rest = rest[: len(runs)], rest[len(runs) :]
    right, out, spread, diag, room, loads, stores, sems = rest
    part = right.shape[1]
    start = pl.multiple_of(column[0] * part, part)
    small = run(
        [
            pltpu.make_async_copy(right_side.at[0, :, pl.ds(start, part)], right, sems.at[0]),
            pltpu.make_async_copy(inverse.at[0, 0], diag, sems.at[1]),
        ]
    )
    sources = (low_blocks, high_blocks)
    reads = run(
        [pltpu.make_async_copy(sources[which].at[0, k], room.at[i], loads.at[i]) for i, (which, k) in enumerate(lines)]
    )
    places = [(j, i) for j, count in enumerate(runs) for i in range(count)]
    writes = [pltpu.make_async_copy(room.at[n], outs[j].at[i], stores.at[n]) for n, (j, i) in enumerate(places)]
    for copy in small:
        copy.wait()
    solved = dot(right[0], diag[...]).astype(BF)
    out[...] = solved
    for i in range(spread.shape[0]):
        spread[i] = solved
    for read, write in zip(reads, writes):
        read.wait()
        write.start()
    for write in writes:
        write.wait()


def begin(lines, runs, column, low_blocks, high_blocks, right_side, inverse, ncol, width):
    block = low_blocks.shape[2:]
    levels, nrhs, size = right_side.shape[1:]
    part = nrhs // ncol
    n = len(lines)
    return pl.pallas_call(
        functools.partial(begin_kernel, lines, runs),
        out_shape=[pltpu.HBM((count,) + block, BF) for count in runs]
        + [jax.ShapeDtypeStruct(shape, BF) for shape in ((levels, part, size), (part, size), (width, part, size))],
        in_specs=[SMEM] + [ANY] * 4,
        out_specs=[ANY] * len(runs) + [VMEM] * 3,
        scratch_shapes=[
            pltpu.VMEM((size, size), BF),
            pltpu.VMEM((n,) + block, BF),
            pltpu.SemaphoreType.DMA((n,)),
            pltpu.SemaphoreType.DMA((n,)),
            pltpu.SemaphoreType.DMA((2,)),
        ],
        compiler_params=params(10),
        name="begin",
    )(column, hbm(low_blocks), hbm(high_blocks), hbm(right_side), hbm(inverse))


def pick(stores, first, place, load):
    width = 32
    at = jnp.maximum(place, 0)
    level, index = at // width - first, at % width
    picked = load(stores[0], index)
    for i in range(1, len(stores)):
        picked = jnp.where(level == i, load(stores[i], index), picked)
    live = (place >= first * width) & (place < (first + len(stores)) * width)
    return jnp.where(live, picked, jnp.zeros_like(picked))


def update_kernel(level, n, extra, table, blocks, *rest):
    stores, rest = rest[:n], rest[n:]
    out = rest[-1]
    ncol, group, part, size = stores[0].shape

    def load(store, index):
        return store[:, index % group].reshape(ncol * part, size)

    total = jnp.zeros((ncol * part, size), F32)
    for slot in range(blocks.shape[2]):
        total += dot(pick(stores, 0, table[level, slot], load), blocks[0, level, slot])
    out[:, :part] = total.reshape(ncol, part, size)
    if extra:
        out[:, part:] = jnp.broadcast_to(rest[0][...][None], (ncol, extra, size))


def update(level, table, blocks, stores, late=None):
    slots, size = blocks.shape[2], blocks.shape[3]
    ncol, group, part, _ = stores[0].shape
    n = len(stores)
    extra = 0 if late is None else late.shape[0]
    return pl.pallas_call(
        functools.partial(update_kernel, level, n, extra),
        out_shape=jax.ShapeDtypeStruct((ncol, part + extra, size), F32),
        in_specs=[SMEM, VMEM] + [VMEM] * (n + (late is not None)),
        out_specs=VMEM,
        compiler_params=params(4),
        cost_estimate=pl.CostEstimate(flops=2 * slots * ncol * part * size * size, bytes_accessed=1 << 20, transcendentals=0),
        name="update",
    )(table, blocks, *stores, *([] if late is None else [late]))


def finish_kernel(level, parts, right, inverse, out, spread, *table):
    residual = right[level]
    part = residual.shape[0]
    if parts is not None:
        total = parts[0, :part]
        for i in range(1, parts.shape[0]):
            total = total + parts[i, :part]
        residual = (residual.astype(F32) - total).astype(BF)
    solved = dot(residual, inverse[0, level]).astype(BF)
    out[...] = solved
    for i in range(spread.shape[0]):
        spread[i] = solved
    if table:
        for i in range(parts.shape[0]):
            table[0][i : i + 1] = parts[i, part : part + 1, :128].astype(I32)


def finish(level, parts, right, inverse, width):
    part, size = right.shape[1:]
    body = functools.partial(finish_kernel, level)
    out_shape = [jax.ShapeDtypeStruct((part, size), BF), jax.ShapeDtypeStruct((width, part, size), BF)]
    if parts is None:
        body = functools.partial(finish_kernel, level, None)
    elif parts.shape[1] > part:
        out_shape.append(jax.ShapeDtypeStruct((parts.shape[0], 128), I32))
    return pl.pallas_call(
        body,
        out_shape=out_shape,
        in_specs=([] if parts is None else [VMEM]) + [VMEM, VMEM],
        out_specs=[VMEM] * len(out_shape),
        compiler_params=params(4),
        cost_estimate=pl.CostEstimate(flops=2 * part * size * size, bytes_accessed=1 << 19, transcendentals=0),
        name="finish",
    )(*([] if parts is None else [parts]), right, inverse)


def row(store, index):
    return store[index]


def older_kernel(first, line, at, newest, levels, table, blocks, *rest):
    inverses, rest = rest[: len(levels)], rest[len(levels) :]
    *stores, out, found, ready, diag, room, sems, ready_sems, end_sems = rest
    ends = fetch_ends(inverses, levels, diag, end_sems)
    ncol, slots = blocks.shape[0], blocks.shape[2]
    cap = ready.shape[0]
    copies = []
    if stores:
        copies = run([pltpu.make_async_copy(blocks.at[c, at], room.at[c], sems.at[c]) for c in range(ncol)])
    n = jnp.int32(0)
    for i in range(ncol * slots):
        place = table[i // slots, line * slots + i % slots]
        hit = (place >= newest * 32) & (place < newest * 32 + 32)

        @pl.when(hit)
        def _():
            found[n] = i * 32 + place - newest * 32

        @pl.when(hit & (n < cap))
        def _():
            pltpu.make_async_copy(blocks.at[i // slots, at, i % slots], ready.at[n], ready_sems.at[n]).start()

        n = n + jnp.where(hit, 1, 0)
    found[ncol * slots] = n
    total = jnp.zeros(out.shape, F32)
    for c, copy in enumerate(copies):
        copy.wait()
        for slot in range(slots):
            total += dot(pick(stores, first, table[c, line * slots + slot], row), room[c, slot])
    out[...] = total

    @pl.loop(0, jnp.minimum(n, cap))
    def _(j):
        pltpu.make_async_copy(blocks.at[0, at, 0], ready.at[j], ready_sems.at[j]).wait()

    for end in ends:
        end.wait()


def older(ready, first, line, at, newest, levels, inverses, table, blocks, stores, part):
    ncol, _, slots, size, _ = blocks.shape
    return pl.pallas_call(
        functools.partial(older_kernel, first, line, at, newest, levels),
        out_shape=[
            pltpu.VMEM((part, size), F32),
            jax.ShapeDtypeStruct((64,), I32),
            pltpu.VMEM((ready, size, size), BF),
            pltpu.VMEM((len(levels), size, size), BF),
        ],
        in_specs=[SMEM, ANY] + [ANY] * len(levels) + [VMEM] * len(stores),
        out_specs=[VMEM, SMEM, VMEM, VMEM],
        scratch_shapes=[
            pltpu.VMEM((ncol if stores else 1, slots, size, size), BF),
            pltpu.SemaphoreType.DMA((ncol,)),
            pltpu.SemaphoreType.DMA((ready,)),
            pltpu.SemaphoreType.DMA((len(levels),)),
        ],
        compiler_params=params(10),
        cost_estimate=pl.CostEstimate(flops=2 * ncol * slots * part * size * size, bytes_accessed=13 << 20, transcendentals=0),
        name="older",
    )(table, hbm(blocks), *[hbm(ref) for ref in inverses], *stores)


def fetch_ends(inverses, levels, diag, sems):
    return run(
        [
            pltpu.make_async_copy(ref.at[0, level], diag.at[i], sems.at[i])
            for i, (ref, level) in enumerate(zip(inverses, levels))
        ]
    )


def finish_row(total, right, level, diag, rest):
    solved = ((right[level] if len(right.shape) > 2 else right[...]).astype(F32) - total).astype(BF)
    for i in range(diag.shape[0]):
        solved = dot(solved, diag[i]).astype(BF)
    for i in range(rest[-1].shape[0]):
        rest[-1][i] = solved
    if len(rest) > 1:
        rest[0][...] = solved


def sparse_kernel(at, level, blocks, store, right, before, found, ready, diag, *rest):
    *rest, room, sems = rest
    ncol, slots = blocks.shape[0], blocks.shape[2]
    cap = ready.shape[0]
    n = found[ncol * slots]

    def fetch(j):
        i = found[j] // 32
        return pltpu.make_async_copy(blocks.at[i // slots, at, i % slots], room.at[j - cap], sems.at[j - cap])

    @pl.loop(cap, jnp.maximum(n, cap))
    def _(j):
        fetch(j).start()

    def some(low, high, load, k, total):
        terms = []
        for u in range(STEP):
            j = low + k * STEP + u
            to = jnp.minimum(j, high - 1)
            picked = store[found[to] % 32]
            picked = jnp.where(j < high, picked, jnp.zeros_like(picked))
            terms.append(dot(picked, load(to)))
        while len(terms) > 1:
            terms = [x + y for x, y in zip(terms[::2], terms[1::2])]
        return total + terms[0]

    held = jnp.minimum(n, cap)
    total = lax.fori_loop(
        0, (held + STEP - 1) // STEP, lambda k, total: some(0, held, lambda j: ready[j], k, total), before[...]
    )

    @pl.loop(cap, jnp.maximum(n, cap))
    def _(j):
        fetch(j).wait()

    more = jnp.maximum(n - cap, 0)
    total = lax.fori_loop(
        0, (more + STEP - 1) // STEP, lambda k, total: some(cap, n, lambda j: room[j - cap], k, total), total
    )
    finish_row(total, right, level, diag, rest)


def solve(at, level, blocks, store, right, before, final=False):
    part, size = right.shape[-2:]
    ncol, slots = blocks.shape[0], blocks.shape[2]
    width = store.shape[0]
    if final:
        out_shape = jax.ShapeDtypeStruct((ncol, part, size), BF)
        out_specs = VMEM
    else:
        out_shape = [jax.ShapeDtypeStruct((part, size), BF), jax.ShapeDtypeStruct((width, part, size), BF)]
        out_specs = [VMEM, VMEM]
    copies = ncol * slots - before[2].shape[0]
    return pl.pallas_call(
        functools.partial(sparse_kernel, at, level),
        out_shape=out_shape,
        in_specs=[ANY, VMEM, VMEM, VMEM, SMEM, VMEM, VMEM],
        out_specs=out_specs,
        scratch_shapes=[
            pltpu.VMEM((copies, size, size), BF),
            pltpu.SemaphoreType.DMA((copies,)),
        ],
        compiler_params=params(10),
        cost_estimate=pl.CostEstimate(flops=2 * ncol * slots * part * size * size, bytes_accessed=4 << 20, transcendentals=0),
        name="solve",
    )(hbm(blocks), store, right, *before)


def shards(
    right_side,
    lower_inverse,
    upper_inverse,
    lower_blocks,
    lower_sources,
    lower_counts,
    upper_blocks,
    upper_sources,
    upper_counts,
):
    width = lax.axis_size(ROW)
    ncol = lax.axis_size(COL)
    group = width // ncol
    column = lax.axis_index(COL)
    levels, nrhs, size = right_side.shape[1:]
    slots = lower_blocks.shape[2]
    part = nrhs // ncol

    last = LAST_SPLIT
    lines = [(0, level - 1) for level in range(last + 1, levels)] + [(1, level) for level in range(levels - 2, -1, -1)]
    head = first_run(lines[: RUNS[0]], lower_blocks, upper_blocks)
    *rows, right, first, copies = begin(
        lines[RUNS[0] :],
        RUNS[1:],
        jnp.full((1,), column, I32),
        lower_blocks,
        upper_blocks,
        right_side,
        lower_inverse,
        ncol,
        width,
    )
    gathered = []
    for count, part_rows in zip(RUNS, [head] + rows):
        whole = lax.all_gather(part_rows, COL, axis=0)
        gathered.extend((whole, i) for i in range(count))

    def places(sources, counts, by_column):
        s, n = sources[0], counts[0]
        live = jnp.arange(slots, dtype=I32)[None] < n
        g = s % width // ncol
        place = s // width * width + g
        if by_column:
            place = (s // width * ncol + s % ncol) * group + g
        return jnp.where(live, place, -1)

    own_table = places(lower_sources, lower_counts, False)
    late = jnp.concatenate(
        [
            places(lower_sources, lower_counts, True)[last:],
            places(upper_sources, upper_counts, True)[::-1],
        ]
    ).reshape(-1)
    late = jnp.pad(late.astype(F32)[None], ((0, 7), (0, size - late.shape[0])))

    def spread(copies):
        return lax.all_to_all(copies, TURNED, 0, 0, tiled=True)

    def by_column(whole):
        return lax.all_to_all(whole.reshape(ncol, group, part, size), COL, 0, 0, tiled=True)

    stores, halves, own = [spread(copies)], [], [first]
    for level in range(1, last + 1):
        halves.append(by_column(stores[-1]))
        partial = update(level - 1, own_table, lower_blocks, halves, late if level == 1 else None)
        parts = lax.all_to_all(partial, COL, 0, 0, tiled=True)
        solved, copies, *rest = finish(level, parts, right, lower_inverse, width)
        if rest:
            table = rest[0]
        own.append(solved)
        if level < last:
            stores.append(spread(copies))

    def step(line, olds, first, newest, levels, inverses, copies):
        blocks, at = gathered[line]
        copies, tied = lax.optimization_barrier((copies, table))
        before = older(READY[line], first, line, at, newest, levels, inverses, tied, blocks, olds, part)
        return spread(copies), before

    line = 0
    for level in range(last + 1, levels):
        ends = [level], [lower_inverse]
        if level == levels - 1:
            ends = [level, level], [lower_inverse, upper_inverse]
        newest, before = step(line, stores, 0, level - 1, *ends, copies)
        blocks, at = gathered[line]
        solved, copies = solve(at, level, blocks, newest, right, before)
        own.append(solved)
        stores.append(newest)
        line += 1
    result, stores = [solved], []
    for level in range(levels - 2, -1, -1):
        newest, before = step(line, stores, level + 2, level + 1, [level], [upper_inverse], copies)
        blocks, at = gathered[line]
        if level == 0:
            done = jnp.broadcast_to(jnp.stack(result)[None], (4, levels - 1, part, size))
            done = lax.all_gather(done, COL, axis=0)[:, 0]
            copies = solve(at, level, blocks, newest, own[level], before, True)
            whole = lax.all_to_all(copies, COL, 0, 0, tiled=True)
        else:
            solved, copies = solve(at, level, blocks, newest, own[level], before)
            result.insert(0, solved)
            stores.insert(0, newest)
        line += 1
    whole = jnp.concatenate([whole[None], jnp.transpose(done, (1, 0, 2, 3))])
    return whole.reshape(1, levels, nrhs, size)


def solution(mesh):
    width, ncol = mesh.devices.shape
    grid = Mesh(mesh.devices.reshape(width // ncol, ncol, ncol // 2, 2), ROW + COL)
    in_specs = (
        P(ROW, None, None, None),
        P(ROW, None, None, None),
        P(ROW, None, None, None),
        P(ROW, None, COL, None, None),
        P(ROW, None, COL),
        P(ROW, None, COL),
        P(ROW, None, COL, None, None),
        P(ROW, None, COL),
        P(ROW, None, COL),
    )
    out_specs = P(ROW, None, None, None)
    return jax.shard_map(shards, mesh=grid, in_specs=in_specs, out_specs=out_specs, check_vma=False)
```

```python
import functools

import jax
import jax.numpy as jnp
from jax import lax
from jax.experimental import pallas as pl
from jax.experimental.pallas import tpu as pltpu
from jax.sharding import Mesh
from jax.sharding import PartitionSpec as P

BF = jnp.bfloat16
F32 = jnp.float32
I32 = jnp.int32
NT = (((1,), (1,)), ((), ()))
ROW = ("g", "z")
TURNED = ("z", "g")
COL = ("x", "core")
SMEM = pl.BlockSpec(memory_space=pltpu.SMEM)
VMEM = pl.BlockSpec(memory_space=pltpu.VMEM)
ANY = pl.BlockSpec(memory_space=pl.ANY)
HBM = pl.BlockSpec(memory_space=pltpu.HBM)
LAST_SPLIT = 3
RUNS = (4, 2, 1)
STEP = 4
READY = (12, 12, 20, 20, 16, 14, 10)


def dot(x, y):
    return lax.dot_general(x, y, NT, preferred_element_type=F32)


def run(copies):
    for copy in copies:
        copy.start()
    return copies


def params(mib):
    return pltpu.CompilerParams(vmem_limit_bytes=mib << 20)


def hbm(blocks):
    return pltpu.with_memory_space_constraint(blocks, pltpu.HBM)


def first_kernel(lines, low_blocks, high_blocks, out, room, loads, stores):
    sources = (low_blocks, high_blocks)
    reads = run(
        [pltpu.make_async_copy(sources[which].at[0, k], room.at[i], loads.at[i]) for i, (which, k) in enumerate(lines)]
    )
    writes = [pltpu.make_async_copy(room.at[i], out.at[i], stores.at[i]) for i in range(len(lines))]
    for read, write in zip(reads, writes):
        read.wait()
        write.start()
    for write in writes:
        write.wait()


def first_run(lines, low_blocks, high_blocks):
    block = low_blocks.shape[2:]
    n = len(lines)
    return pl.pallas_call(
        functools.partial(first_kernel, lines),
        out_shape=pltpu.HBM((n,) + block, BF),
        in_specs=[ANY] * 2,
        out_specs=ANY,
        scratch_shapes=[
            pltpu.VMEM((n,) + block, BF),
            pltpu.SemaphoreType.DMA((n,)),
            pltpu.SemaphoreType.DMA((n,)),
        ],
        compiler_params=params(10),
        name="first",
    )(hbm(low_blocks), hbm(high_blocks))


def begin_kernel(lines, runs, column, low_blocks, high_blocks, right_side, inverse, *rest):
    outs, rest = rest[: len(runs)], rest[len(runs) :]
    right, out, spread, diag, room, loads, stores, sems = rest
    part = right.shape[1]
    start = pl.multiple_of(column[0] * part, part)
    small = run(
        [
            pltpu.make_async_copy(right_side.at[0, :, pl.ds(start, part)], right, sems.at[0]),
            pltpu.make_async_copy(inverse.at[0, 0], diag, sems.at[1]),
        ]
    )
    sources = (low_blocks, high_blocks)
    reads = run(
        [pltpu.make_async_copy(sources[which].at[0, k], room.at[i], loads.at[i]) for i, (which, k) in enumerate(lines)]
    )
    places = [(j, i) for j, count in enumerate(runs) for i in range(count)]
    writes = [pltpu.make_async_copy(room.at[n], outs[j].at[i], stores.at[n]) for n, (j, i) in enumerate(places)]
    for copy in small:
        copy.wait()
    solved = dot(right[0], diag[...]).astype(BF)
    out[...] = solved
    for i in range(spread.shape[0]):
        spread[i] = solved
    for read, write in zip(reads, writes):
        read.wait()
        write.start()
    for write in writes:
        write.wait()


def begin(lines, runs, column, low_blocks, high_blocks, right_side, inverse, ncol, width):
    block = low_blocks.shape[2:]
    levels, nrhs, size = right_side.shape[1:]
    part = nrhs // ncol
    n = len(lines)
    return pl.pallas_call(
        functools.partial(begin_kernel, lines, runs),
        out_shape=[pltpu.HBM((count,) + block, BF) for count in runs]
        + [jax.ShapeDtypeStruct(shape, BF) for shape in ((levels, part, size), (part, size), (width, part, size))],
        in_specs=[SMEM] + [ANY] * 4,
        out_specs=[ANY] * len(runs) + [VMEM] * 3,
        scratch_shapes=[
            pltpu.VMEM((size, size), BF),
            pltpu.VMEM((n,) + block, BF),
            pltpu.SemaphoreType.DMA((n,)),
            pltpu.SemaphoreType.DMA((n,)),
            pltpu.SemaphoreType.DMA((2,)),
        ],
        compiler_params=params(10),
        name="begin",
    )(column, hbm(low_blocks), hbm(high_blocks), hbm(right_side), hbm(inverse))


def pick(stores, first, place, load):
    width = 32
    at = jnp.maximum(place, 0)
    level, index = at // width - first, at % width
    picked = load(stores[0], index)
    for i in range(1, len(stores)):
        picked = jnp.where(level == i, load(stores[i], index), picked)
    live = (place >= first * width) & (place < (first + len(stores)) * width)
    return jnp.where(live, picked, jnp.zeros_like(picked))


def update_kernel(level, n, extra, table, blocks, *rest):
    stores, rest = rest[:n], rest[n:]
    out = rest[-1]
    ncol, group, part, size = stores[0].shape

    def load(store, index):
        return store[:, index % group].reshape(ncol * part, size)

    total = jnp.zeros((ncol * part, size), F32)
    for slot in range(blocks.shape[2]):
        total += dot(pick(stores, 0, table[level, slot], load), blocks[0, level, slot])
    out[:, :part] = total.reshape(ncol, part, size).astype(BF)
    if extra:
        out[:, part:] = jnp.broadcast_to(rest[0][...][None], (ncol, extra, size))


def update(level, table, blocks, stores, late=None):
    slots, size = blocks.shape[2], blocks.shape[3]
    ncol, group, part, _ = stores[0].shape
    n = len(stores)
    extra = 0 if late is None else late.shape[0]
    return pl.pallas_call(
        functools.partial(update_kernel, level, n, extra),
        out_shape=jax.ShapeDtypeStruct((ncol, part + extra, size), BF),
        in_specs=[SMEM, VMEM] + [VMEM] * (n + (late is not None)),
        out_specs=VMEM,
        compiler_params=params(4),
        cost_estimate=pl.CostEstimate(flops=2 * slots * ncol * part * size * size, bytes_accessed=1 << 20, transcendentals=0),
        name="update",
    )(table, blocks, *stores, *([] if late is None else [late]))


def finish_kernel(level, parts, right, inverse, out, spread, *table):
    residual = right[level]
    part = residual.shape[0]
    if parts is not None:
        total = parts[0, :part].astype(F32)
        for i in range(1, parts.shape[0]):
            total = total + parts[i, :part].astype(F32)
        residual = (residual.astype(F32) - total).astype(BF)
    solved = dot(residual, inverse[0, level]).astype(BF)
    out[...] = solved
    for i in range(spread.shape[0]):
        spread[i] = solved
    if table:
        for i in range(parts.shape[0]):
            table[0][i : i + 1] = parts[i, part : part + 1, :128].astype(F32).astype(I32)


def finish(level, parts, right, inverse, width):
    part, size = right.shape[1:]
    body = functools.partial(finish_kernel, level)
    out_shape = [jax.ShapeDtypeStruct((part, size), BF), jax.ShapeDtypeStruct((width, part, size), BF)]
    if parts is None:
        body = functools.partial(finish_kernel, level, None)
    elif parts.shape[1] > part:
        out_shape.append(jax.ShapeDtypeStruct((parts.shape[0], 128), I32))
    return pl.pallas_call(
        body,
        out_shape=out_shape,
        in_specs=([] if parts is None else [VMEM]) + [VMEM, VMEM],
        out_specs=[VMEM] * len(out_shape),
        compiler_params=params(4),
        cost_estimate=pl.CostEstimate(flops=2 * part * size * size, bytes_accessed=1 << 19, transcendentals=0),
        name="finish",
    )(*([] if parts is None else [parts]), right, inverse)


def row(store, index):
    return store[index]


def older_kernel(first, line, at, newest, levels, table, blocks, *rest):
    inverses, rest = rest[: len(levels)], rest[len(levels) :]
    *stores, out, found, ready, diag, room, sems, ready_sems, end_sems = rest
    ends = fetch_ends(inverses, levels, diag, end_sems)
    ncol, slots = blocks.shape[0], blocks.shape[2]
    cap = ready.shape[0]
    copies = []
    if stores:
        copies = run([pltpu.make_async_copy(blocks.at[c, at], room.at[c], sems.at[c]) for c in range(ncol)])
    n = jnp.int32(0)
    for i in range(ncol * slots):
        place = table[i // slots, line * slots + i % slots]
        hit = (place >= newest * 32) & (place < newest * 32 + 32)

        @pl.when(hit)
        def _():
            found[n] = i * 32 + place - newest * 32

        @pl.when(hit & (n < cap))
        def _():
            pltpu.make_async_copy(blocks.at[i // slots, at, i % slots], ready.at[n], ready_sems.at[n]).start()

        n = n + jnp.where(hit, 1, 0)
    found[ncol * slots] = n
    total = jnp.zeros(out.shape, F32)
    for c, copy in enumerate(copies):
        copy.wait()
        for slot in range(slots):
            total += dot(pick(stores, first, table[c, line * slots + slot], row), room[c, slot])
    out[...] = total

    @pl.loop(0, jnp.minimum(n, cap))
    def _(j):
        pltpu.make_async_copy(blocks.at[0, at, 0], ready.at[j], ready_sems.at[j]).wait()

    for end in ends:
        end.wait()


def older(ready, first, line, at, newest, levels, inverses, table, blocks, stores, part):
    ncol, _, slots, size, _ = blocks.shape
    return pl.pallas_call(
        functools.partial(older_kernel, first, line, at, newest, levels),
        out_shape=[
            pltpu.VMEM((part, size), F32),
            jax.ShapeDtypeStruct((64,), I32),
            pltpu.VMEM((ready, size, size), BF),
            pltpu.VMEM((len(levels), size, size), BF),
        ],
        in_specs=[SMEM, ANY] + [ANY] * len(levels) + [VMEM] * len(stores),
        out_specs=[VMEM, SMEM, VMEM, VMEM],
        scratch_shapes=[
            pltpu.VMEM((ncol if stores else 1, slots, size, size), BF),
            pltpu.SemaphoreType.DMA((ncol,)),
            pltpu.SemaphoreType.DMA((ready,)),
            pltpu.SemaphoreType.DMA((len(levels),)),
        ],
        compiler_params=params(10),
        cost_estimate=pl.CostEstimate(flops=2 * ncol * slots * part * size * size, bytes_accessed=13 << 20, transcendentals=0),
        name="older",
    )(table, hbm(blocks), *[hbm(ref) for ref in inverses], *stores)


def fetch_ends(inverses, levels, diag, sems):
    return run(
        [
            pltpu.make_async_copy(ref.at[0, level], diag.at[i], sems.at[i])
            for i, (ref, level) in enumerate(zip(inverses, levels))
        ]
    )


def finish_row(total, right, level, diag, rest):
    solved = ((right[level] if len(right.shape) > 2 else right[...]).astype(F32) - total).astype(BF)
    for i in range(diag.shape[0]):
        solved = dot(solved, diag[i]).astype(BF)
    if len(rest) > 2:
        *done, out = rest
        for i in range(out.shape[0]):
            out[i, 0] = solved
            for j, ref in enumerate(done):
                out[i, j + 1] = ref[...]
    else:
        out, spread = rest
        out[...] = solved
        for i in range(spread.shape[0]):
            spread[i] = solved


def sparse_kernel(at, level, blocks, store, right, before, found, ready, diag, *rest):
    *rest, room, sems = rest
    ncol, slots = blocks.shape[0], blocks.shape[2]
    cap = ready.shape[0]
    n = found[ncol * slots]

    def fetch(j):
        i = found[j] // 32
        return pltpu.make_async_copy(blocks.at[i // slots, at, i % slots], room.at[j - cap], sems.at[j - cap])

    @pl.loop(cap, jnp.maximum(n, cap))
    def _(j):
        fetch(j).start()

    def some(low, high, load, k, total):
        terms = []
        for u in range(STEP):
            j = low + k * STEP + u
            to = jnp.minimum(j, high - 1)
            picked = store[found[to] % 32]
            picked = jnp.where(j < high, picked, jnp.zeros_like(picked))
            terms.append(dot(picked, load(to)))
        while len(terms) > 1:
            terms = [x + y for x, y in zip(terms[::2], terms[1::2])]
        return total + terms[0]

    held = jnp.minimum(n, cap)
    total = lax.fori_loop(
        0, (held + STEP - 1) // STEP, lambda k, total: some(0, held, lambda j: ready[j], k, total), before[...]
    )

    @pl.loop(cap, jnp.maximum(n, cap))
    def _(j):
        fetch(j).wait()

    more = jnp.maximum(n - cap, 0)
    total = lax.fori_loop(
        0, (more + STEP - 1) // STEP, lambda k, total: some(cap, n, lambda j: room[j - cap], k, total), total
    )
    finish_row(total, right, level, diag, rest)


def solve(at, level, blocks, store, right, before, done=()):
    part, size = right.shape[-2:]
    ncol, slots = blocks.shape[0], blocks.shape[2]
    width = store.shape[0]
    if done:
        out_shape = jax.ShapeDtypeStruct((ncol, len(done) + 1, part, size), BF)
        out_specs = VMEM
    else:
        out_shape = [jax.ShapeDtypeStruct((part, size), BF), jax.ShapeDtypeStruct((width, part, size), BF)]
        out_specs = [VMEM, VMEM]
    copies = ncol * slots - before[2].shape[0]
    return pl.pallas_call(
        functools.partial(sparse_kernel, at, level),
        out_shape=out_shape,
        in_specs=[ANY, VMEM, VMEM, VMEM, SMEM, VMEM, VMEM] + [VMEM] * len(done),
        out_specs=out_specs,
        scratch_shapes=[
            pltpu.VMEM((copies, size, size), BF),
            pltpu.SemaphoreType.DMA((copies,)),
        ],
        compiler_params=params(10),
        cost_estimate=pl.CostEstimate(flops=2 * ncol * slots * part * size * size, bytes_accessed=4 << 20, transcendentals=0),
        name="solve",
    )(hbm(blocks), store, right, *before, *done)


def shards(
    right_side,
    lower_inverse,
    upper_inverse,
    lower_blocks,
    lower_sources,
    lower_counts,
    upper_blocks,
    upper_sources,
    upper_counts,
):
    width = lax.axis_size(ROW)
    ncol = lax.axis_size(COL)
    group = width // ncol
    column = lax.axis_index(COL)
    levels, nrhs, size = right_side.shape[1:]
    slots = lower_blocks.shape[2]
    part = nrhs // ncol

    last = LAST_SPLIT
    lines = [(0, level - 1) for level in range(last + 1, levels)] + [(1, level) for level in range(levels - 2, -1, -1)]
    head = first_run(lines[: RUNS[0]], lower_blocks, upper_blocks)
    *rows, right, first, copies = begin(
        lines[RUNS[0] :],
        RUNS[1:],
        jnp.full((1,), column, I32),
        lower_blocks,
        upper_blocks,
        right_side,
        lower_inverse,
        ncol,
        width,
    )
    gathered = []
    for count, part_rows in zip(RUNS, [head] + rows):
        whole = lax.all_gather(part_rows, COL, axis=0)
        gathered.extend((whole, i) for i in range(count))

    def places(sources, counts, by_column):
        s, n = sources[0], counts[0]
        live = jnp.arange(slots, dtype=I32)[None] < n
        g = s % width // ncol
        place = s // width * width + g
        if by_column:
            place = (s // width * ncol + s % ncol) * group + g
        return jnp.where(live, place, -1)

    own_table = places(lower_sources, lower_counts, False)
    late = jnp.concatenate(
        [
            places(lower_sources, lower_counts, True)[last:],
            places(upper_sources, upper_counts, True)[::-1],
        ]
    ).reshape(-1)
    late = jnp.pad(late.astype(BF)[None], ((0, 15), (0, size - late.shape[0])))

    def spread(copies):
        return lax.all_to_all(copies, TURNED, 0, 0, tiled=True)

    def by_column(whole):
        return lax.all_to_all(whole.reshape(ncol, group, part, size), COL, 0, 0, tiled=True)

    stores, halves, own = [spread(copies)], [], [first]
    for level in range(1, last + 1):
        halves.append(by_column(stores[-1]))
        partial = update(level - 1, own_table, lower_blocks, halves, late if level == 1 else None)
        parts = lax.all_to_all(partial, COL, 0, 0, tiled=True)
        solved, copies, *rest = finish(level, parts, right, lower_inverse, width)
        if rest:
            table = rest[0]
        own.append(solved)
        if level < last:
            stores.append(spread(copies))

    def step(line, olds, first, newest, levels, inverses, copies):
        blocks, at = gathered[line]
        copies, tied = lax.optimization_barrier((copies, table))
        before = older(READY[line], first, line, at, newest, levels, inverses, tied, blocks, olds, part)
        return spread(copies), before

    line = 0
    for level in range(last + 1, levels):
        ends = [level], [lower_inverse]
        if level == levels - 1:
            ends = [level, level], [lower_inverse, upper_inverse]
        newest, before = step(line, stores, 0, level - 1, *ends, copies)
        blocks, at = gathered[line]
        solved, copies = solve(at, level, blocks, newest, right, before)
        own.append(solved)
        stores.append(newest)
        line += 1
    result, stores = [solved], []
    for level in range(levels - 2, -1, -1):
        newest, before = step(line, stores, level + 2, level + 1, [level], [upper_inverse], copies)
        blocks, at = gathered[line]
        if level == 0:
            whole = lax.all_to_all(solve(at, level, blocks, newest, own[level], before, result), COL, 0, 0, tiled=True)
        else:
            solved, copies = solve(at, level, blocks, newest, own[level], before)
            result.insert(0, solved)
            stores.insert(0, newest)
        line += 1
    return jnp.transpose(whole, (1, 0, 2, 3)).reshape(1, levels, nrhs, size)


def solution(mesh):
    width, ncol = mesh.devices.shape
    grid = Mesh(mesh.devices.reshape(width // ncol, ncol, ncol // 2, 2), ROW + COL)
    in_specs = (
        P(ROW, None, None, None),
        P(ROW, None, None, None),
        P(ROW, None, None, None),
        P(ROW, None, COL, None, None),
        P(ROW, None, COL),
        P(ROW, None, COL),
        P(ROW, None, COL, None, None),
        P(ROW, None, COL),
        P(ROW, None, COL),
    )
    out_specs = P(ROW, None, None, None)
    return jax.shard_map(shards, mesh=grid, in_specs=in_specs, out_specs=out_specs, check_vma=False)
```
